128 devices in a mesh: lat: 8 (over y, core), lon: 16 (over x, z).
Axes of the slice: x: 4, y: 4, z: 4, core: 2. Of those that a mesh axis runs over, the one named last changes fastest.
Arguments:
- state: float32 [4, 80, 64, 2048], P(None, None, 'lat', 'lon'), may hold values from -4 to 4
- mixing: float32 [64, 2048], P('lat', 'lon'), may hold values from 0.2 to 5
- insolation: float32 [64, 2048], P('lat', 'lon'), may hold values from 0 to 1
- filter_rows: int32 [64], replicated, may hold values 0 or 1
- block_map: int32 [64, 2048], P('lat', 'lon'), may hold values from 0 to 131071, as said below
Outputs:
- state_out: float32 [4, 80, 64, 2048], P(None, None, 'lat', 'lon')
- block_heating: float32 [128, 80, 1024], P(('lat', 'lon'))
The draws below stay inside these ranges and needn't reach their ends.
Inputs may be any that keep to these rules, and one draw needn't show every extreme that they name: `block_map`: blocks are numbered like the devices of the lat+lon axes. The 1024 columns of every device's tile give exactly 8 columns to each block, and each block's 1024 slots are each named by exactly one column.
All inputs are finite; a program needn't handle non-finite values.
Results may differ from the reference program's by a relative error of at most 0.0001.
Values sent between devices are 32-bit elements; how exact they have to be, the bound alone decides.
No kernel may reach another device: no remote copies, remote signals or barrier semaphores. Data moves between devices by JAX's collectives and lax.ppermute only.
A program may use at most 64 MiB of HBM per device.

```python
import math
import jax
import jax.numpy as jnp
from jax import lax

FIELDS = 4
LEV = 80
CLAT = 8
CLON = 128
STEPS = 2
KEEP = 64
NLAT = 64
NLON = 2048
N_LAT = 8
N_LON = 16


def draw_block_map(key, part):
    devices = N_LAT * N_LON
    columns = CLAT * CLON
    per_peer = columns // devices
    source_keys = jax.random.split(jax.random.fold_in(key, 11), devices)
    source_perms = jax.vmap(lambda single: jax.random.permutation(single, columns))(source_keys).astype(jnp.int32)
    target = source_perms // per_peer
    position = source_perms % per_peer
    source_ids = jnp.arange(devices, dtype=jnp.int32)[:, None]
    pair_index = source_ids * per_peer + position
    target_keys = jax.random.split(jax.random.fold_in(key, 12), devices)
    target_perms = jax.vmap(lambda single: jax.random.permutation(single, columns))(target_keys).astype(jnp.int32)
    slots = target_perms[target, pair_index]
    values = target * columns + slots
    shaped = values.reshape(N_LAT, N_LON, CLAT, CLON)
    return jnp.transpose(shaped, (0, 2, 1, 3)).reshape(N_LAT * CLAT, N_LON * CLON).astype(jnp.int32)


def plant(entries, rng, least, largest):
    shape = entries.shape
    spot = [jax.random.randint(jax.random.fold_in(rng, axis), (), 0, shape[axis]) for axis in range(len(shape))]
    entries = entries.at[tuple(spot)].set(least)
    longest = shape.index(max(shape))
    spot[longest] = (spot[longest] + 1) % shape[longest]
    return entries.at[tuple(spot)].set(largest)


def steps_of(rng, extent, cuts, low, largest):
    def one(axis_at, shards_of):
        steps = jax.random.uniform(jax.random.fold_in(jax.random.fold_in(rng, 6), axis_at), (shards_of,), jnp.float32, low / len(cuts), largest / len(cuts))
        return jnp.repeat(jnp.exp(steps), extent[axis_at] // shards_of).reshape((-1,) + (1,) * (len(extent) - axis_at - 1))

    loudness = one(*cuts[0])
    for cut in cuts[1:]:
        loudness = loudness * one(*cut)
    return loudness


def noise(stream_key, extent, spread, limit, shards=(), kind=jnp.bfloat16):
    values = spread * jax.random.normal(stream_key, extent, jnp.float32)
    if shards:
        values = values * steps_of(stream_key, extent, shards, -0.22, 0.18)
    return jnp.clip(values, -limit, limit).astype(kind)


def setup_inputs(seed: int = 0) -> dict:
    keys = jax.random.split(jax.random.key(seed), 6)
    return {
        "state": noise(keys[0], (FIELDS, LEV, NLAT, NLON), 1.0, 4.0, ((2, 8), (3, 16)), jnp.float32),
        "mixing": jnp.clip(jnp.exp(math.log(5.0) - 3.218876 * jax.random.uniform(keys[1], (NLAT, NLON), jnp.float32) ** steps_of(keys[1], (NLAT, NLON), ((0, 8), (1, 16)), -0.2, 0.2)), 0.2, 5.0),
        "insolation": jnp.clip(1.0 * jax.random.uniform(keys[2], (NLAT, NLON), jnp.float32) ** steps_of(keys[2], (NLAT, NLON), ((0, 8), (1, 16)), -0.2, 0.2), 0.0, 1.0),
        "filter_rows": plant((jax.random.randint(keys[3], (NLAT,), 0, 3) < 1).astype(jnp.int32), jax.random.fold_in(keys[3], 1), 0, 1),
        "block_map": draw_block_map(jax.random.fold_in(keys[5], 71), 0),
    }


ADVECT = 0.1
DIFFUSE = 0.1
ROTATE = 0.2
RADIATE = 0.5
FLOOR = 0.25


def advance(extended, row_index, total_rows):
    center = extended[:, :, 1:-1, 1:-1]
    eastern = extended[:, :, 1:-1, 2:]
    western = extended[:, :, 1:-1, :-2]
    northern = extended[:, :, 2:, 1:-1]
    southern = extended[:, :, :-2, 1:-1]
    latitude = (row_index.astype(jnp.float32) + 0.5) * (math.pi / total_rows) - 0.5 * math.pi
    metric = (1.0 / jnp.maximum(jnp.cos(latitude), FLOOR))[:, None]
    coriolis = jnp.sin(latitude)[:, None]
    zonal_wind = center[0]
    meridional = center[1]
    stepped = center - ADVECT * (zonal_wind * metric * (eastern - western) + meridional * (northern - southern))
    stepped = stepped + DIFFUSE * (eastern + western + northern + southern - 4.0 * center)
    zonal_new = stepped[0] + ROTATE * coriolis * meridional
    meridional_new = stepped[1] - ROTATE * coriolis * zonal_wind
    return jnp.concatenate([zonal_new[None], meridional_new[None], stepped[2:]], axis=0)


def mix_columns(column_fields, column_mix):
    levels = column_fields.shape[1]
    level_ids = jnp.arange(levels)
    at_end = jnp.where((level_ids == 0) | (level_ids == levels - 1), 1.0, 0.0).astype(column_fields.dtype)
    by_level = jnp.moveaxis(column_fields, 1, 0)

    def forward(carry, inputs):
        upper_ratio, upper_value = carry
        level_value, end_flag = inputs
        diagonal = 1.0 + (2.0 - end_flag) * column_mix
        denominator = diagonal + column_mix * upper_ratio
        ratio = -column_mix / denominator
        value = (level_value + column_mix * upper_value) / denominator
        return (ratio, value), (ratio, value)

    start = (jnp.zeros_like(column_mix), jnp.zeros_like(by_level[0]))
    unused, (ratios, values) = lax.scan(forward, start, (by_level, at_end))

    def backward(below, inputs):
        ratio, value = inputs
        solved = value - ratio * below
        return solved, solved

    unused_last, solved = lax.scan(backward, jnp.zeros_like(by_level[0]), (ratios, values), reverse=True)
    return jnp.moveaxis(solved, 0, 1)


def physics(column_fields, column_mix, column_sun):
    solved = mix_columns(column_fields, column_mix)
    warmed = solved[2] + RADIATE * column_sun * solved[3]
    heating = warmed - column_fields[2]
    return jnp.stack([solved[0], solved[1], warmed, solved[3]]), heating


def reference(state, mixing, insolation, filter_rows, block_map):
    fields, levels, total_rows, total_cols = state.shape
    row_index = jnp.arange(total_rows)
    current = state
    for round_index in range(STEPS):
        beside_all = jnp.concatenate([current[..., -1:], current, current[..., :1]], axis=3)
        beside_all = jnp.pad(beside_all, ((0, 0), (0, 0), (1, 1), (0, 0)))
        stepped = advance(beside_all, row_index, total_rows)
        spectrum = jnp.fft.rfft(stepped, axis=3)
        keep_mask = jnp.arange(spectrum.shape[3]) < KEEP
        spectrum = jnp.where(keep_mask, spectrum, jnp.zeros_like(spectrum))
        smooth = jnp.fft.irfft(spectrum, n=total_cols, axis=3).astype(stepped.dtype)
        current = jnp.where(filter_rows[None, None, :, None] == 1, smooth, stepped)
    flattened = current.reshape(fields, levels, total_rows * total_cols)
    mixed_state, heating = physics(flattened, mixing.reshape(-1), insolation.reshape(-1))
    state_out = mixed_state.reshape(state.shape)
    devices = N_LAT * N_LON
    columns = total_rows * total_cols // devices
    block_table = jnp.zeros((levels, devices * columns), heating.dtype).at[:, block_map.reshape(-1)].set(heating)
    block_heating = jnp.transpose(block_table.reshape(levels, devices, columns), (1, 0, 2))
    return state_out, block_heating
```

```python
import math

import jax
import jax.numpy as jnp
import numpy as np
from jax import lax
from jax.experimental import pallas as pl
from jax.experimental.pallas import tpu as pltpu
from jax.sharding import PartitionSpec as P

KEEP = 64
ADVECT = 0.1
DIFFUSE = 0.1
ROTATE = 0.2
RADIATE = 0.5
FLOOR = 0.25

FIELDS = 4
LEVELS = 80
ROWS = 8
COLS = 128
N_LAT = 8
N_LON = 16
GROUP = LEVELS // N_LON
PAIRS = FIELDS * GROUP
MAIN = PAIRS * ROWS
EDGE = 2 * PAIRS
EDGE_PAD = 48
ALL = MAIN + EDGE_PAD
COLUMNS = ROWS * COLS
BLOCKS = N_LAT * N_LON
CIRCLE = COLS * N_LON

F32 = jnp.float32
BF16 = jnp.bfloat16
VMEM = pl.BlockSpec(memory_space=pltpu.VMEM)
SMEM = pl.BlockSpec(memory_space=pltpu.SMEM)


def halves(values):
    high = values.astype(BF16)
    low = (values - high.astype(F32)).astype(BF16)
    return high, low


def fourier_tables():
    waves = np.arange(KEEP)
    phase = 2.0 * math.pi / CIRCLE * (np.outer(np.arange(CIRCLE), waves) % CIRCLE)
    analysis = np.concatenate([np.cos(phase), np.sin(phase)], axis=1)
    weights = np.where(waves == 0, 1.0, 2.0)[:, None] / CIRCLE
    synthesis = np.concatenate([weights * np.cos(phase.T), weights * np.sin(phase.T)], axis=0)

    def split(table, axis):
        high = table.astype(BF16)
        low = (table - high.astype(np.float64)).astype(BF16)
        return np.concatenate([high, low], axis=axis)

    return split(analysis, 1), split(synthesis, 0)


def row_tables():
    total = N_LAT * ROWS
    table = np.zeros((N_LAT, 8, ROWS, COLS), np.float32)
    rows = np.arange(-1, total + 1)
    latitude = (rows + 0.5) * (math.pi / total) - 0.5 * math.pi
    metric = 1.0 / np.maximum(np.cos(latitude), FLOOR)
    coriolis = np.sin(latitude)
    for band in range(N_LAT):
        first = band * ROWS
        table[band, 0] = metric[first + 1 : first + 1 + ROWS, None]
        table[band, 1] = coriolis[first + 1 : first + 1 + ROWS, None]
        table[band, 2] = metric[first + 1 + ROWS]
        table[band, 3] = coriolis[first + 1 + ROWS]
        table[band, 4] = float(band < N_LAT - 1)
        table[band, 5] = metric[first]
        table[band, 6] = coriolis[first]
        table[band, 7] = float(band > 0)
    return table


def pack_kernel(state_ref, low_ref, high_ref):
    for tile in range(N_LON):
        for place, row in enumerate((0, 1)):
            low_ref[tile, pl.ds(place * PAIRS, PAIRS), :] = state_ref[
                tile, pl.ds(row, PAIRS, stride=ROWS), :
            ]
        for place, row in enumerate((ROWS - 2, ROWS - 1)):
            high_ref[tile, pl.ds(place * PAIRS, PAIRS), :] = state_ref[
                tile, pl.ds(row, PAIRS, stride=ROWS), :
            ]


def stencil(center, east, west, north, south, zonal, meridional, metric):
    stepped = center - ADVECT * (
        zonal * metric * (east - west) + meridional * (north - south)
    )
    return stepped + DIFFUSE * (east + west + north + south - 4.0 * center)


def turned(field, zonal, meridional, coriolis):
    if field == 0:
        return ROTATE * coriolis * meridional
    if field == 1:
        return -ROTATE * coriolis * zonal
    return None


def dynamics_kernel(
    band_ref, filter_ref, state_ref, north_ref, south_ref, rows_ref, analysis_ref, synthesis_ref,
    out_ref, stepped_ref, current_ref, split_ref,
):
    band = band_ref[0]
    first = band * ROWS
    lane = lax.broadcasted_iota(jnp.int32, (ROWS, COLS), 1)
    sub = lax.broadcasted_iota(jnp.int32, (ROWS, COLS), 0)
    lane_edge = lane[:GROUP]
    metric = rows_ref[band, 0]
    coriolis = rows_ref[band, 1]

    def beside(load, tile, lanes):
        here = load(tile)
        after = load((tile + 1) % N_LON)
        before = load((tile - 1) % N_LON)
        east = jnp.where(
            lanes == COLS - 1, pltpu.roll(after, COLS - 1, 1), pltpu.roll(here, COLS - 1, 1)
        )
        west = jnp.where(lanes == 0, pltpu.roll(before, 1, 1), pltpu.roll(here, 1, 1))
        return here, east, west

    def step_main(source, north_of, south_of):
        def level_step(level, carry):
            for field in range(FIELDS):
                at = pl.ds(pl.multiple_of((field * GROUP + level) * ROWS, ROWS), ROWS)
                at_u = pl.ds(pl.multiple_of(level * ROWS, ROWS), ROWS)
                at_v = pl.ds(pl.multiple_of((GROUP + level) * ROWS, ROWS), ROWS)
                pair = field * GROUP + level
                for tile in range(N_LON):
                    here, east, west = beside(lambda t: source[t, at, :], tile, lane)
                    north = jnp.where(
                        sub == ROWS - 1, north_of(tile, pair), pltpu.roll(here, ROWS - 1, 0)
                    )
                    south = jnp.where(sub == 0, south_of(tile, pair), pltpu.roll(here, 1, 0))
                    zonal = source[tile, at_u, :]
                    meridional = source[tile, at_v, :]
                    result = stencil(here, east, west, north, south, zonal, meridional, metric)
                    extra = turned(field, zonal, meridional, coriolis)
                    if extra is not None:
                        result = result + extra
                    stepped_ref[tile, at, :] = result
            return carry

        lax.fori_loop(0, GROUP, level_step, 0)

    def step_edge(side):
        base = 2 + 3 * side
        metric_edge = rows_ref[band, base][:GROUP]
        coriolis_edge = rows_ref[band, base + 1][:GROUP]
        exists = rows_ref[band, base + 2][:GROUP]
        halo = (north_ref, south_ref)[side]
        near = (0, PAIRS)[side]
        far = (PAIRS, 0)[side]
        for tile in range(N_LON):
            zonal = halo[tile, near : near + GROUP, :]
            meridional = halo[tile, near + GROUP : near + 2 * GROUP, :]
            for field in range(FIELDS):
                at = near + field * GROUP
                here, east, west = beside(lambda t: halo[t, at : at + GROUP, :], tile, lane_edge)
                outer = halo[tile, far + field * GROUP : far + (field + 1) * GROUP, :]
                inner = state_ref[
                    tile,
                    pl.ds(field * GROUP * ROWS + (ROWS - 1, 0)[side], GROUP, stride=ROWS),
                    :,
                ]
                north, south = ((outer, inner), (inner, outer))[side]
                result = stencil(
                    here, east, west, north, south, zonal, meridional, metric_edge
                )
                extra = turned(field, zonal, meridional, coriolis_edge)
                if extra is not None:
                    result = result + extra
                place = MAIN + side * PAIRS + field * GROUP
                stepped_ref[tile, place : place + GROUP, :] = jnp.where(exists > 0.5, result, 0.0)

    wanted = jnp.zeros((ROWS, COLS), jnp.int32)
    for row in range(ROWS):
        wanted = jnp.where(sub == row, filter_ref[first + row], wanted)
    wanted_main = jnp.concatenate([wanted] * PAIRS, axis=0) == 1
    wanted_above = filter_ref[jnp.minimum(first + ROWS, N_LAT * ROWS - 1)]
    wanted_below = filter_ref[jnp.maximum(first - 1, 0)]
    edge_row = lax.broadcasted_iota(jnp.int32, (EDGE_PAD, COLS), 0)
    wanted_edge = jnp.where(edge_row < PAIRS, wanted_above, wanted_below) == 1

    def polar_filter(rows, target):
        for tile in range(N_LON):
            high, low = halves(stepped_ref[tile, :rows, :])
            split_ref[:rows, tile * COLS : (tile + 1) * COLS] = high
            split_ref[rows : 2 * rows, tile * COLS : (tile + 1) * COLS] = low
        sums = jnp.dot(split_ref[: 2 * rows, :], analysis_ref[...], preferred_element_type=F32)
        sums = sums[:rows] + sums[rows:]
        sums = sums[:, :COLS] + sums[:, COLS:]
        high, low = halves(sums)
        both = jnp.concatenate(
            [jnp.concatenate([high, high], axis=1), jnp.concatenate([low, low], axis=1)], axis=0
        )
        for pair in range(N_LON // 2):
            smooth = jnp.dot(
                both,
                synthesis_ref[:, pair * 2 * COLS : (pair + 1) * 2 * COLS],
                preferred_element_type=F32,
            )
            smooth = smooth[:rows] + smooth[rows:]
            for side in range(2):
                tile = 2 * pair + side
                piece = smooth[:, side * COLS : (side + 1) * COLS]
                target[tile, :MAIN, :] = jnp.where(
                    wanted_main, piece[:MAIN], stepped_ref[tile, :MAIN, :]
                )
                if rows > MAIN:
                    target[tile, MAIN:rows, :] = jnp.where(
                        wanted_edge, piece[MAIN:], stepped_ref[tile, MAIN:rows, :]
                    )

    stepped_ref[:, MAIN + EDGE :, :] = jnp.zeros((N_LON, ALL - MAIN - EDGE, COLS), F32)
    step_main(
        state_ref,
        lambda tile, pair: north_ref[tile, pl.ds(pair, 1), :],
        lambda tile, pair: south_ref[tile, pl.ds(PAIRS + pair, 1), :],
    )
    step_edge(0)
    step_edge(1)
    polar_filter(ALL, current_ref)
    step_main(
        current_ref,
        lambda tile, pair: current_ref[tile, pl.ds(MAIN + pair, 1), :],
        lambda tile, pair: current_ref[tile, pl.ds(MAIN + PAIRS + pair, 1), :],
    )
    polar_filter(MAIN, out_ref)


def prepare_kernel(mixing_ref, map_ref, gain_ref, inverse_ref, order_ref):
    mix = mixing_ref[...]

    def level_step(level, above):
        inside = jnp.where((level == 0) | (level == LEVELS - 1), 1.0, 2.0)
        inverse = 1.0 / (1.0 + inside * mix - mix * above)
        gain = mix * inverse
        gain_ref[level] = gain
        inverse_ref[level] = inverse
        return gain

    lax.fori_loop(0, LEVELS, level_step, jnp.zeros_like(mix))

    target = map_ref[...] // COLUMNS
    before = lax.broadcasted_iota(jnp.int32, (COLS, 2 * COLS), 0)
    after = lax.broadcasted_iota(jnp.int32, (COLS, 2 * COLS), 1)
    counter = jnp.where((before < after) | (after >= COLS), 1.0, 0.0).astype(BF16)
    block = lax.broadcasted_iota(jnp.int32, (BLOCKS, COLS), 0)
    place = lax.broadcasted_iota(jnp.int32, (COLUMNS, COLS), 0)
    earlier = jnp.zeros((BLOCKS, COLS), F32)
    for row in range(ROWS):
        goal = target[row : row + 1, :]
        chosen = jnp.where(block == goal, 1.0, 0.0)
        counted = jnp.dot(chosen.astype(BF16), counter, preferred_element_type=F32)
        rank = jnp.sum(chosen * (counted[:, :COLS] + earlier), axis=0, keepdims=True)
        earlier = earlier + counted[:, COLS:]
        seat = goal * ROWS + rank.astype(jnp.int32)
        order_ref[:, row * COLS : (row + 1) * COLS] = jnp.where(place == seat, 1.0, 0.0).astype(BF16)


def physics_kernel(
    dyn_ref, mixing_ref, sun_ref, map_ref, gain_ref, inverse_ref, order_ref,
    out_ref, send_ref, heating_ref, table_ref,
):
    zero = jnp.zeros((ROWS, COLS), F32)

    def forward(group, carry):
        for inner in range(GROUP):
            level = group * GROUP + inner
            gain = gain_ref[level]
            inverse = inverse_ref[level]
            carry = tuple(
                dyn_ref[group, (field * GROUP + inner) * ROWS : (field * GROUP + inner + 1) * ROWS, :]
                * inverse
                + gain * carry[field]
                for field in range(FIELDS)
            )
            for field in range(FIELDS):
                out_ref[field, level] = carry[field]
        return carry

    lax.fori_loop(0, N_LON, forward, (zero,) * FIELDS)
    sun = RADIATE * sun_ref[...]

    def backward(step, carry):
        group = N_LON - 1 - step
        for inner in reversed(range(GROUP)):
            level = group * GROUP + inner
            gain = gain_ref[level]
            carry = tuple(out_ref[field, level] + gain * carry[field] for field in range(FIELDS))
            warmed = carry[2] + sun * carry[3]
            out_ref[0, level] = carry[0]
            out_ref[1, level] = carry[1]
            out_ref[2, level] = warmed
            out_ref[3, level] = carry[3]
            at = (2 * GROUP + inner) * ROWS
            heating_ref[pl.ds(pl.multiple_of(level * ROWS, ROWS), ROWS), :] = (
                warmed - dyn_ref[group, at : at + ROWS, :]
            )
        return carry

    lax.fori_loop(0, N_LON, backward, (zero,) * FIELDS)

    slots = (map_ref[...] % COLUMNS).astype(F32)
    top = lax.broadcasted_iota(jnp.int32, (COLS - LEVELS, COLS), 0) == 0
    for row in range(ROWS):
        body = heating_ref[pl.ds(row, LEVELS, stride=ROWS), :]
        tail = jnp.where(top, slots[row : row + 1, :], 0.0)
        high, low = halves(jnp.concatenate([body, tail], axis=0))
        table_ref[:COLS, row * COLS : (row + 1) * COLS] = high
        table_ref[COLS:, row * COLS : (row + 1) * COLS] = low
    sent = lax.dot_general(
        order_ref[...], table_ref[...], (((1,), (1,)), ((), ())), preferred_element_type=F32
    )
    send_ref[...] = sent[:, :COLS] + sent[:, COLS:]


def place_kernel(got_ref, out_ref):
    got = got_ref[...]
    slot = got[:, LEVELS : LEVELS + 1]
    column = lax.broadcasted_iota(jnp.int32, (COLUMNS, COLUMNS), 1).astype(F32)
    chosen = jnp.where(column == slot, 1.0, 0.0).astype(BF16)
    high, low = halves(got.T[:LEVELS])
    both = jnp.concatenate([high, low], axis=0)
    placed = jnp.dot(both, chosen, preferred_element_type=F32)
    out_ref[0] = placed[:LEVELS] + placed[LEVELS:]


def per_device(state, mixing, insolation, filter_rows, block_map):
    analysis, synthesis = (jnp.asarray(table) for table in fourier_tables())
    rows = jnp.asarray(row_tables())
    band = lax.axis_index("lat").astype(jnp.int32).reshape(1)
    up = [(i, i + 1) for i in range(N_LAT - 1)]
    down = [(i + 1, i) for i in range(N_LAT - 1)]

    by_group = state.reshape(FIELDS, N_LON, GROUP, ROWS, COLS).transpose(1, 0, 2, 3, 4)
    circles = lax.all_to_all(
        by_group.reshape(N_LON, MAIN, COLS), "lon", split_axis=0, concat_axis=0, tiled=True
    )
    edge = jax.ShapeDtypeStruct((N_LON, EDGE, COLS), F32)
    first_rows, last_rows = pl.pallas_call(
        pack_kernel, out_shape=(edge, edge), in_specs=[VMEM], out_specs=(VMEM, VMEM), name="pack"
    )(circles)
    north = lax.ppermute(first_rows, "lat", down)
    south = lax.ppermute(last_rows, "lat", up)
    dyn = pl.pallas_call(
        dynamics_kernel,
        out_shape=jax.ShapeDtypeStruct((N_LON, MAIN, COLS), F32),
        in_specs=[SMEM, SMEM] + [VMEM] * 6,
        out_specs=VMEM,
        scratch_shapes=[
            pltpu.VMEM((N_LON, ALL, COLS), F32),
            pltpu.VMEM((N_LON, ALL, COLS), F32),
            pltpu.VMEM((2 * ALL, CIRCLE), BF16),
        ],
        name="dynamics",
    )(band, filter_rows, circles, north, south, rows, analysis, synthesis)
    levels = jax.ShapeDtypeStruct((LEVELS, ROWS, COLS), F32)
    gain, inverse, order = pl.pallas_call(
        prepare_kernel,
        out_shape=(levels, levels, jax.ShapeDtypeStruct((COLUMNS, COLUMNS), BF16)),
        in_specs=[VMEM] * 2,
        out_specs=(VMEM,) * 3,
        name="prepare",
    )(mixing, block_map)
    columns = lax.all_to_all(dyn, "lon", split_axis=0, concat_axis=0, tiled=True)
    new_state, sent = pl.pallas_call(
        physics_kernel,
        out_shape=(
            jax.ShapeDtypeStruct((FIELDS, LEVELS, ROWS, COLS), F32),
            jax.ShapeDtypeStruct((COLUMNS, COLS), F32),
        ),
        in_specs=[VMEM] * 7,
        out_specs=(VMEM,) * 2,
        scratch_shapes=[
            pltpu.VMEM((LEVELS * ROWS, COLS), F32),
            pltpu.VMEM((2 * COLS, COLUMNS), BF16),
        ],
        name="physics",
    )(columns, mixing, insolation, block_map, gain, inverse, order)
    got = lax.all_to_all(
        sent.reshape(BLOCKS, ROWS, COLS), ("lat", "lon"), split_axis=0, concat_axis=0, tiled=True
    )
    block_heating = pl.pallas_call(
        place_kernel,
        out_shape=jax.ShapeDtypeStruct((1, LEVELS, COLUMNS), F32),
        in_specs=[VMEM],
        out_specs=VMEM,
        name="place",
    )(got.reshape(COLUMNS, COLS))
    return new_state, block_heating


def solution(mesh):
    in_specs = (P(None, None, "lat", "lon"), P("lat", "lon"), P("lat", "lon"), P(), P("lat", "lon"))
    out_specs = (P(None, None, "lat", "lon"), P(("lat", "lon"), None, None))
    return jax.shard_map(
        per_device, mesh=mesh, in_specs=in_specs, out_specs=out_specs, check_vma=False
    )
```

```python
import math

import jax
import jax.numpy as jnp
import numpy as np
from jax import lax
from jax.experimental import pallas as pl
from jax.experimental.pallas import tpu as pltpu
from jax.sharding import PartitionSpec as P

KEEP = 64
ADVECT = 0.1
DIFFUSE = 0.1
ROTATE = 0.2
RADIATE = 0.5
FLOOR = 0.25

FIELDS = 4
LEVELS = 80
ROWS = 8
COLS = 128
N_LAT = 8
N_LON = 16
GROUP = LEVELS // N_LON
PAIRS = FIELDS * GROUP
MAIN = PAIRS * ROWS
EDGE = 2 * PAIRS
EDGE_PAD = 48
ALL = MAIN + EDGE_PAD
COLUMNS = ROWS * COLS
BLOCKS = N_LAT * N_LON
CIRCLE = COLS * N_LON

F32 = jnp.float32
BF16 = jnp.bfloat16
VMEM = pl.BlockSpec(memory_space=pltpu.VMEM)
ANY = pl.BlockSpec(memory_space=pl.ANY)
SMEM = pl.BlockSpec(memory_space=pltpu.SMEM)


def call(kernel, name, out_shapes, scratch, megabytes, *args, scalars=0, stored=(), after=()):
    def body(*refs):
        kernel(*refs[: len(args)], *refs[len(args) + len(after) :])

    placed = args[:scalars] + tuple(
        pltpu.with_memory_space_constraint(arg, pltpu.VMEM) for arg in args[scalars:]
    )
    return pl.pallas_call(
        body,
        out_shape=tuple(
            jax.ShapeDtypeStruct(shape, kind) if index in stored else pltpu.VMEM(shape, kind)
            for index, (shape, kind) in enumerate(out_shapes)
        ),
        in_specs=[SMEM] * scalars + [VMEM] * (len(args) - scalars) + [ANY] * len(after),
        out_specs=(VMEM,) * len(out_shapes),
        scratch_shapes=scratch,
        compiler_params=pltpu.CompilerParams(vmem_limit_bytes=megabytes << 20),
        name=name,
    )(*placed, *after)


def halves(values):
    high = values.astype(BF16)
    low = (values - high.astype(F32)).astype(BF16)
    return high, low


def fourier_tables():
    waves = np.arange(KEEP)
    phase = 2.0 * math.pi / CIRCLE * (np.outer(np.arange(CIRCLE), waves) % CIRCLE)
    analysis = np.concatenate([np.cos(phase), np.sin(phase)], axis=1)
    weights = np.where(waves == 0, 1.0, 2.0)[:, None] / CIRCLE
    synthesis = np.concatenate([weights * np.cos(phase.T), weights * np.sin(phase.T)], axis=0)

    def split(table, axis):
        high = table.astype(BF16)
        low = (table - high.astype(np.float64)).astype(BF16)
        return np.concatenate([high, low], axis=axis)

    return split(analysis, 1), split(synthesis, 0)


def row_tables():
    total = N_LAT * ROWS
    table = np.zeros((N_LAT, 8, ROWS, COLS), np.float32)
    rows = np.arange(-1, total + 1)
    latitude = (rows + 0.5) * (math.pi / total) - 0.5 * math.pi
    metric = 1.0 / np.maximum(np.cos(latitude), FLOOR)
    coriolis = np.sin(latitude)
    for band in range(N_LAT):
        first = band * ROWS
        table[band, 0] = metric[first + 1 : first + 1 + ROWS, None]
        table[band, 1] = coriolis[first + 1 : first + 1 + ROWS, None]
        table[band, 2] = metric[first + 1 + ROWS]
        table[band, 3] = coriolis[first + 1 + ROWS]
        table[band, 4] = float(band < N_LAT - 1)
        table[band, 5] = metric[first]
        table[band, 6] = coriolis[first]
        table[band, 7] = float(band > 0)
    return table


def pack_kernel(band_ref, state_ref, near_ref, far_ref):
    odd = band_ref[0] % 2
    near_row = (ROWS - 2) * (1 - odd)
    far_row = (ROWS - 2) * odd
    for tile in range(N_LON):
        for ref, row in ((near_ref, near_row), (far_ref, far_row)):
            for place in range(2):
                ref[tile, pl.ds(place * PAIRS, PAIRS), :] = state_ref[
                    tile, pl.ds(row + place, PAIRS, stride=ROWS), :
                ]


def weights(zonal, meridional, metric):
    along = ADVECT * (zonal * metric)
    across = ADVECT * meridional
    return DIFFUSE - along, DIFFUSE + along, DIFFUSE - across, DIFFUSE + across


def stencil(center, east, west, north, south, shares):
    to_east, to_west, to_north, to_south = shares
    return (
        (1.0 - 4.0 * DIFFUSE) * center
        + (to_east * east + to_west * west)
        + (to_north * north + to_south * south)
    )


def turned(field, zonal, meridional, coriolis):
    if field == 0:
        return ROTATE * coriolis * meridional
    if field == 1:
        return -ROTATE * coriolis * zonal
    return None


def dynamics_kernel(
    band_ref, filter_ref, state_ref, near_ref, far_ref, rows_ref, analysis_ref, synthesis_ref,
    out_ref, north_ref, south_ref, stepped_ref, current_ref, split_ref,
):
    band = band_ref[0]
    first = band * ROWS
    lane = lax.broadcasted_iota(jnp.int32, (ROWS, COLS), 1)
    sub = lax.broadcasted_iota(jnp.int32, (ROWS, COLS), 0)
    lane_edge = lane[:GROUP]
    metric = rows_ref[band, 0]
    coriolis = rows_ref[band, 1]

    even = lax.broadcasted_iota(jnp.int32, (EDGE, COLS), 0) * 0 + band % 2 == 0
    for tile in range(N_LON):
        near_rows = near_ref[tile]
        far_rows = far_ref[tile]
        north_ref[tile] = jnp.where(even, near_rows, far_rows)
        south_ref[tile] = jnp.where(even, far_rows, near_rows)

    def beside(load, tile, lanes):
        here = load(tile)
        after = load((tile + 1) % N_LON)
        before = load((tile - 1) % N_LON)
        east = jnp.where(
            lanes == COLS - 1, pltpu.roll(after, COLS - 1, 1), pltpu.roll(here, COLS - 1, 1)
        )
        west = jnp.where(lanes == 0, pltpu.roll(before, 1, 1), pltpu.roll(here, 1, 1))
        return here, east, west

    def step_main(source, north_of, south_of):
        def level_step(level, carry):
            def at(field):
                return pl.ds(pl.multiple_of((field * GROUP + level) * ROWS, ROWS), ROWS)

            for tile in range(N_LON):
                zonal = source[tile, at(0), :]
                meridional = source[tile, at(1), :]
                shares = weights(zonal, meridional, metric)
                for field in range(FIELDS):
                    pair = field * GROUP + level
                    here, east, west = beside(lambda t: source[t, at(field), :], tile, lane)
                    north = jnp.where(
                        sub == ROWS - 1, north_of(tile, pair), pltpu.roll(here, ROWS - 1, 0)
                    )
                    south = jnp.where(sub == 0, south_of(tile, pair), pltpu.roll(here, 1, 0))
                    result = stencil(here, east, west, north, south, shares)
                    extra = turned(field, zonal, meridional, coriolis)
                    if extra is not None:
                        result = result + extra
                    stepped_ref[tile, at(field), :] = result
            return carry

        lax.fori_loop(0, GROUP, level_step, 0)

    def step_edge(side):
        base = 2 + 3 * side
        metric_edge = rows_ref[band, base][:GROUP]
        coriolis_edge = rows_ref[band, base + 1][:GROUP]
        exists = rows_ref[band, base + 2][:GROUP]
        halo = (north_ref, south_ref)[side]
        near = (0, PAIRS)[side]
        far = (PAIRS, 0)[side]
        for tile in range(N_LON):
            zonal = halo[tile, near : near + GROUP, :]
            meridional = halo[tile, near + GROUP : near + 2 * GROUP, :]
            shares = weights(zonal, meridional, metric_edge)
            for field in range(FIELDS):
                at = near + field * GROUP
                here, east, west = beside(lambda t: halo[t, at : at + GROUP, :], tile, lane_edge)
                outer = halo[tile, far + field * GROUP : far + (field + 1) * GROUP, :]
                inner = state_ref[
                    tile,
                    pl.ds(field * GROUP * ROWS + (ROWS - 1, 0)[side], GROUP, stride=ROWS),
                    :,
                ]
                north, south = ((outer, inner), (inner, outer))[side]
                result = stencil(here, east, west, north, south, shares)
                extra = turned(field, zonal, meridional, coriolis_edge)
                if extra is not None:
                    result = result + extra
                place = MAIN + side * PAIRS + field * GROUP
                stepped_ref[tile, place : place + GROUP, :] = jnp.where(exists > 0.5, result, 0.0)

    wanted = jnp.zeros((ROWS, COLS), jnp.int32)
    for row in range(ROWS):
        wanted = jnp.where(sub == row, filter_ref[first + row], wanted)
    wanted_main = jnp.concatenate([wanted] * PAIRS, axis=0) == 1
    wanted_above = filter_ref[jnp.minimum(first + ROWS, N_LAT * ROWS - 1)]
    wanted_below = filter_ref[jnp.maximum(first - 1, 0)]
    edge_row = lax.broadcasted_iota(jnp.int32, (EDGE_PAD, COLS), 0)
    wanted_edge = jnp.where(edge_row < PAIRS, wanted_above, wanted_below) == 1

    def polar_filter(rows, target):
        for tile in range(N_LON):
            high, low = halves(stepped_ref[tile, :rows, :])
            split_ref[:rows, tile * COLS : (tile + 1) * COLS] = high
            split_ref[rows : 2 * rows, tile * COLS : (tile + 1) * COLS] = low
        sums = jnp.dot(split_ref[: 2 * rows, :], analysis_ref[...], preferred_element_type=F32)
        sums = sums[:rows] + sums[rows:]
        sums = sums[:, :COLS] + sums[:, COLS:]
        high, low = halves(sums)
        both = jnp.concatenate(
            [jnp.concatenate([high, high], axis=1), jnp.concatenate([low, low], axis=1)], axis=0
        )
        for pair in range(N_LON // 2):
            smooth = jnp.dot(
                both,
                synthesis_ref[:, pair * 2 * COLS : (pair + 1) * 2 * COLS],
                preferred_element_type=F32,
            )
            smooth = smooth[:rows] + smooth[rows:]
            for side in range(2):
                tile = 2 * pair + side
                piece = smooth[:, side * COLS : (side + 1) * COLS]
                target[tile, :MAIN, :] = jnp.where(
                    wanted_main, piece[:MAIN], stepped_ref[tile, :MAIN, :]
                )
                if rows > MAIN:
                    target[tile, MAIN:rows, :] = jnp.where(
                        wanted_edge, piece[MAIN:], stepped_ref[tile, MAIN:rows, :]
                    )

    stepped_ref[:, MAIN + EDGE :, :] = jnp.zeros((N_LON, ALL - MAIN - EDGE, COLS), F32)
    step_main(
        state_ref,
        lambda tile, pair: north_ref[tile, pl.ds(pair, 1), :],
        lambda tile, pair: south_ref[tile, pl.ds(PAIRS + pair, 1), :],
    )
    step_edge(0)
    step_edge(1)
    polar_filter(ALL, current_ref)
    step_main(
        current_ref,
        lambda tile, pair: current_ref[tile, pl.ds(MAIN + pair, 1), :],
        lambda tile, pair: current_ref[tile, pl.ds(MAIN + PAIRS + pair, 1), :],
    )
    polar_filter(MAIN, out_ref)


def prepare_kernel(mixing_ref, map_ref, gain_ref, inverse_ref, order_ref):
    mix = mixing_ref[...]

    def level_step(level, above):
        inside = jnp.where((level == 0) | (level == LEVELS - 1), 1.0, 2.0)
        inverse = 1.0 / (1.0 + inside * mix - mix * above)
        gain = mix * inverse
        gain_ref[level] = gain
        inverse_ref[level] = inverse
        return gain

    lax.fori_loop(0, LEVELS, level_step, jnp.zeros_like(mix))

    target = map_ref[...] // COLUMNS
    before = lax.broadcasted_iota(jnp.int32, (COLS, 2 * COLS), 0)
    after = lax.broadcasted_iota(jnp.int32, (COLS, 2 * COLS), 1)
    counter = jnp.where((before < after) | (after >= COLS), 1.0, 0.0).astype(BF16)
    block = lax.broadcasted_iota(jnp.int32, (BLOCKS, COLS), 0)
    place = lax.broadcasted_iota(jnp.int32, (COLUMNS, COLS), 0)
    earlier = jnp.zeros((BLOCKS, COLS), F32)
    for row in range(ROWS):
        goal = target[row : row + 1, :]
        chosen = jnp.where(block == goal, 1.0, 0.0)
        counted = jnp.dot(chosen.astype(BF16), counter, preferred_element_type=F32)
        rank = jnp.sum(chosen * (counted[:, :COLS] + earlier), axis=0, keepdims=True)
        earlier = earlier + counted[:, COLS:]
        seat = goal * ROWS + rank.astype(jnp.int32)
        order_ref[:, row * COLS : (row + 1) * COLS] = jnp.where(place == seat, 1.0, 0.0).astype(BF16)


def physics_kernel(
    dyn_ref, mixing_ref, sun_ref, map_ref, gain_ref, inverse_ref, order_ref,
    out_ref, send_ref, heating_ref, table_ref,
):
    zero = jnp.zeros((ROWS, COLS), F32)

    def forward(group, carry):
        for inner in range(GROUP):
            level = group * GROUP + inner
            gain = gain_ref[level]
            inverse = inverse_ref[level]
            carry = tuple(
                dyn_ref[group, (field * GROUP + inner) * ROWS : (field * GROUP + inner + 1) * ROWS, :]
                * inverse
                + gain * carry[field]
                for field in range(FIELDS)
            )
            for field in range(FIELDS):
                out_ref[field, level] = carry[field]
        return carry

    lax.fori_loop(0, N_LON, forward, (zero,) * FIELDS)
    sun = RADIATE * sun_ref[...]

    def backward(step, carry):
        group = N_LON - 1 - step
        for inner in reversed(range(GROUP)):
            level = group * GROUP + inner
            gain = gain_ref[level]
            carry = tuple(out_ref[field, level] + gain * carry[field] for field in range(FIELDS))
            warmed = carry[2] + sun * carry[3]
            out_ref[0, level] = carry[0]
            out_ref[1, level] = carry[1]
            out_ref[2, level] = warmed
            out_ref[3, level] = carry[3]
            at = (2 * GROUP + inner) * ROWS
            heating_ref[pl.ds(pl.multiple_of(level * ROWS, ROWS), ROWS), :] = (
                warmed - dyn_ref[group, at : at + ROWS, :]
            )
        return carry

    lax.fori_loop(0, N_LON, backward, (zero,) * FIELDS)

    slots = (map_ref[...] % COLUMNS).astype(F32)
    top = lax.broadcasted_iota(jnp.int32, (COLS - LEVELS, COLS), 0) == 0
    for row in range(ROWS):
        body = heating_ref[pl.ds(row, LEVELS, stride=ROWS), :]
        tail = jnp.where(top, slots[row : row + 1, :], 0.0)
        high, low = halves(jnp.concatenate([body, tail], axis=0))
        table_ref[:COLS, row * COLS : (row + 1) * COLS] = high
        table_ref[COLS:, row * COLS : (row + 1) * COLS] = low
    sent = lax.dot_general(
        order_ref[...], table_ref[...], (((1,), (1,)), ((), ())), preferred_element_type=F32
    )
    send_ref[...] = sent[:, :COLS] + sent[:, COLS:]


def place_kernel(got_ref, out_ref):
    got = got_ref[...]
    slot = got[:, LEVELS : LEVELS + 1]
    column = lax.broadcasted_iota(jnp.int32, (COLUMNS, COLUMNS), 1).astype(F32)
    chosen = jnp.where(column == slot, 1.0, 0.0).astype(BF16)
    high, low = halves(got.T[:LEVELS])
    both = jnp.concatenate([high, low], axis=0)
    placed = jnp.dot(both, chosen, preferred_element_type=F32)
    out_ref[0] = placed[:LEVELS] + placed[LEVELS:]


def per_device(state, mixing, insolation, filter_rows, block_map):
    analysis, synthesis = (jnp.asarray(table) for table in fourier_tables())
    rows = jnp.asarray(row_tables())
    band = lax.axis_index("lat").astype(jnp.int32).reshape(1)

    state, band = lax.optimization_barrier((state, band))
    by_group = state.reshape(FIELDS, N_LON, GROUP, ROWS, COLS).transpose(1, 0, 2, 3, 4)
    circles = lax.all_to_all(
        by_group.reshape(N_LON, MAIN, COLS), "lon", split_axis=0, concat_axis=0, tiled=True
    )
    edge = ((N_LON, EDGE, COLS), F32)
    to_near, to_far = call(pack_kernel, "pack", (edge, edge), [], 4, band, circles, scalars=1)
    near = lax.ppermute(to_near, "lat", [(i, i ^ 1) for i in range(N_LAT)])
    far = lax.ppermute(
        to_far, "lat", [(i, ((i + 1) ^ 1) - 1) for i in range(1, N_LAT - 1)]
    )
    levels = ((LEVELS, ROWS, COLS), F32)
    gain, inverse, order = call(
        prepare_kernel, "prepare", (levels, levels, ((COLUMNS, COLUMNS), BF16)), [], 4,
        mixing, block_map,
        after=(to_near,),
    )
    (dyn,) = call(
        dynamics_kernel,
        "dynamics",
        (((N_LON, MAIN, COLS), F32),),
        [
            pltpu.VMEM((N_LON, EDGE, COLS), F32),
            pltpu.VMEM((N_LON, EDGE, COLS), F32),
            pltpu.VMEM((N_LON, ALL, COLS), F32),
            pltpu.VMEM((N_LON, ALL, COLS), F32),
            pltpu.VMEM((2 * ALL, CIRCLE), BF16),
        ],
        16,
        band, filter_rows, circles, near, far, rows, analysis, synthesis,
        scalars=2,
        after=(gain,),
    )
    columns = lax.all_to_all(dyn, "lon", split_axis=0, concat_axis=0, tiled=True)
    new_state, sent = call(
        physics_kernel,
        "physics",
        (((FIELDS, LEVELS, ROWS, COLS), F32), ((COLUMNS, COLS), F32)),
        [pltpu.VMEM((LEVELS * ROWS, COLS), F32), pltpu.VMEM((2 * COLS, COLUMNS), BF16)],
        12,
        columns, mixing, insolation, block_map, gain, inverse, order,
        stored=(),
    )
    got = lax.all_to_all(
        sent.reshape(BLOCKS, ROWS, COLS), ("lat", "lon"), split_axis=0, concat_axis=0, tiled=True
    )
    (block_heating,) = call(
        place_kernel, "place", (((1, LEVELS, COLUMNS), F32),), [], 8, got.reshape(COLUMNS, COLS),
        stored=(0,),
    )
    return new_state, block_heating


def solution(mesh):
    in_specs = (P(None, None, "lat", "lon"), P("lat", "lon"), P("lat", "lon"), P(), P("lat", "lon"))
    out_specs = (P(None, None, "lat", "lon"), P(("lat", "lon"), None, None))
    return jax.shard_map(
        per_device, mesh=mesh, in_specs=in_specs, out_specs=out_specs, check_vma=False
    )
```

```python
import math

import jax
import jax.numpy as jnp
import numpy as np
from jax import lax
from jax.experimental import pallas as pl
from jax.experimental.pallas import tpu as pltpu
from jax.sharding import PartitionSpec as P

KEEP = 64
ADVECT = 0.1
DIFFUSE = 0.1
ROTATE = 0.2
RADIATE = 0.5
FLOOR = 0.25

FIELDS = 4
LEVELS = 80
ROWS = 8
COLS = 128
N_LAT = 8
N_LON = 16
GROUP = LEVELS // N_LON
PAIRS = FIELDS * GROUP
MAIN = PAIRS * ROWS
EDGE = 2 * PAIRS
EDGE_PAD = 48
ALL = MAIN + EDGE_PAD
COLUMNS = ROWS * COLS
BLOCKS = N_LAT * N_LON
CIRCLE = COLS * N_LON

F32 = jnp.float32
BF16 = jnp.bfloat16
VMEM = pl.BlockSpec(memory_space=pltpu.VMEM)
ANY = pl.BlockSpec(memory_space=pl.ANY)
SMEM = pl.BlockSpec(memory_space=pltpu.SMEM)


def call(kernel, name, out_shapes, scratch, megabytes, *args, scalars=0, stored=(), after=()):
    def body(*refs):
        kernel(*refs[: len(args)], *refs[len(args) + len(after) :])

    placed = args[:scalars] + tuple(
        pltpu.with_memory_space_constraint(arg, pltpu.VMEM) for arg in args[scalars:]
    )
    return pl.pallas_call(
        body,
        out_shape=tuple(
            jax.ShapeDtypeStruct(shape, kind) if index in stored else pltpu.VMEM(shape, kind)
            for index, (shape, kind) in enumerate(out_shapes)
        ),
        in_specs=[SMEM] * scalars + [VMEM] * (len(args) - scalars) + [ANY] * len(after),
        out_specs=(VMEM,) * len(out_shapes),
        scratch_shapes=scratch,
        compiler_params=pltpu.CompilerParams(vmem_limit_bytes=megabytes << 20),
        name=name,
    )(*placed, *after)


def halves(values):
    high = values.astype(BF16)
    low = (values - high.astype(F32)).astype(BF16)
    return high, low


def fourier_tables():
    waves = np.arange(KEEP)
    phase = 2.0 * math.pi / CIRCLE * (np.outer(np.arange(CIRCLE), waves) % CIRCLE)
    analysis = np.concatenate([np.cos(phase), np.sin(phase)], axis=1)
    weights = np.where(waves == 0, 1.0, 2.0)[:, None] / CIRCLE
    synthesis = np.concatenate([weights * np.cos(phase.T), weights * np.sin(phase.T)], axis=0)

    def split(table, axis):
        high = table.astype(BF16)
        low = (table - high.astype(np.float64)).astype(BF16)
        return np.concatenate([high, low], axis=axis)

    return split(analysis, 1), split(synthesis, 0)


def row_tables():
    total = N_LAT * ROWS
    table = np.zeros((N_LAT, 8, ROWS, COLS), np.float32)
    rows = np.arange(-1, total + 1)
    latitude = (rows + 0.5) * (math.pi / total) - 0.5 * math.pi
    metric = 1.0 / np.maximum(np.cos(latitude), FLOOR)
    coriolis = np.sin(latitude)
    for band in range(N_LAT):
        first = band * ROWS
        table[band, 0] = metric[first + 1 : first + 1 + ROWS, None]
        table[band, 1] = coriolis[first + 1 : first + 1 + ROWS, None]
        table[band, 2] = metric[first + 1 + ROWS]
        table[band, 3] = coriolis[first + 1 + ROWS]
        table[band, 4] = float(band < N_LAT - 1)
        table[band, 5] = metric[first]
        table[band, 6] = coriolis[first]
        table[band, 7] = float(band > 0)
    return table


def pack_kernel(band_ref, state_ref, near_ref, far_ref):
    odd = band_ref[0] % 2
    near_row = (ROWS - 2) * (1 - odd)
    far_row = (ROWS - 2) * odd
    for tile in range(N_LON):
        for ref, row in ((near_ref, near_row), (far_ref, far_row)):
            for place in range(2):
                ref[tile, pl.ds(place * PAIRS, PAIRS), :] = state_ref[
                    tile, pl.ds(row + place, PAIRS, stride=ROWS), :
                ]


def weights(zonal, meridional, metric):
    along = ADVECT * (zonal * metric)
    across = ADVECT * meridional
    return DIFFUSE - along, DIFFUSE + along, DIFFUSE - across, DIFFUSE + across


def stencil(center, east, west, north, south, shares):
    to_east, to_west, to_north, to_south = shares
    return (
        (1.0 - 4.0 * DIFFUSE) * center
        + (to_east * east + to_west * west)
        + (to_north * north + to_south * south)
    )


def turned(field, zonal, meridional, coriolis):
    if field == 0:
        return ROTATE * coriolis * meridional
    if field == 1:
        return -ROTATE * coriolis * zonal
    return None


def neighbours(load, lanes):
    kept = {}

    def rolled(tile, shift):
        tile = tile % N_LON
        if (tile, shift) not in kept:
            kept[tile, shift] = pltpu.roll(load(tile), shift, 1)
        return kept[tile, shift]

    def beside(tile):
        east = jnp.where(lanes == COLS - 1, rolled(tile + 1, COLS - 1), rolled(tile, COLS - 1))
        west = jnp.where(lanes == 0, rolled(tile - 1, 1), rolled(tile, 1))
        return load(tile), east, west

    return beside


def step_main(source, target, north_of, south_of, metric, coriolis):
    lane = lax.broadcasted_iota(jnp.int32, (ROWS, COLS), 1)
    sub = lax.broadcasted_iota(jnp.int32, (ROWS, COLS), 0)

    def level_step(level, carry):
        def at(field):
            return pl.ds(pl.multiple_of((field * GROUP + level) * ROWS, ROWS), ROWS)

        def reader(field):
            kept = {}

            def load(tile):
                if tile not in kept:
                    kept[tile] = source[tile, at(field), :]
                return kept[tile]

            return load

        beside = [neighbours(reader(field), lane) for field in range(FIELDS)]
        for tile in range(N_LON):
            zonal = source[tile, at(0), :]
            meridional = source[tile, at(1), :]
            shares = weights(zonal, meridional, metric)
            for field in range(FIELDS):
                pair = field * GROUP + level
                here, east, west = beside[field](tile)
                north = jnp.where(
                    sub == ROWS - 1, north_of(tile, pair), pltpu.roll(here, ROWS - 1, 0)
                )
                south = jnp.where(sub == 0, south_of(tile, pair), pltpu.roll(here, 1, 0))
                result = stencil(here, east, west, north, south, shares)
                extra = turned(field, zonal, meridional, coriolis)
                if extra is not None:
                    result = result + extra
                target[tile, at(field), :] = result
        return carry

    lax.fori_loop(0, GROUP, level_step, 0)


def inside_kernel(band_ref, state_ref, rows_ref, out_ref):
    band = band_ref[0]
    step_main(
        state_ref, out_ref, lambda tile, pair: 0.0, lambda tile, pair: 0.0,
        rows_ref[band, 0], rows_ref[band, 1],
    )


def dynamics_kernel(
    band_ref, filter_ref, state_ref, inside_ref, near_ref, far_ref, rows_ref, analysis_ref, synthesis_ref,
    out_ref, north_ref, south_ref, stepped_ref, current_ref, split_ref,
):
    band = band_ref[0]
    first = band * ROWS
    sub = lax.broadcasted_iota(jnp.int32, (ROWS, COLS), 0)
    lane_edge = lax.broadcasted_iota(jnp.int32, (GROUP, COLS), 1)
    metric = rows_ref[band, 0]
    coriolis = rows_ref[band, 1]

    even = lax.broadcasted_iota(jnp.int32, (EDGE, COLS), 0) * 0 + band % 2 == 0
    for tile in range(N_LON):
        near_rows = near_ref[tile]
        far_rows = far_ref[tile]
        north_ref[tile] = jnp.where(even, near_rows, far_rows)
        south_ref[tile] = jnp.where(even, far_rows, near_rows)

    def step_edge(side):
        base = 2 + 3 * side
        metric_edge = rows_ref[band, base][:GROUP]
        coriolis_edge = rows_ref[band, base + 1][:GROUP]
        exists = rows_ref[band, base + 2][:GROUP]
        halo = (north_ref, south_ref)[side]
        near = (0, PAIRS)[side]
        far = (PAIRS, 0)[side]
        own = (ROWS - 1, 0)[side]
        beside = [
            neighbours(
                lambda t, at=near + field * GROUP: halo[t, at : at + GROUP, :], lane_edge
            )
            for field in range(FIELDS)
        ]
        for tile in range(N_LON):
            zonal = halo[tile, near : near + GROUP, :]
            meridional = halo[tile, near + GROUP : near + 2 * GROUP, :]
            shares = weights(zonal, meridional, metric_edge)
            own_wind = state_ref[tile, pl.ds(GROUP * ROWS + own, GROUP, stride=ROWS), :]
            given = DIFFUSE + (-ADVECT, ADVECT)[side] * own_wind
            for field in range(FIELDS):
                own_rows = pl.ds(field * GROUP * ROWS + own, GROUP, stride=ROWS)
                here, east, west = beside[field](tile)
                outer = halo[tile, far + field * GROUP : far + (field + 1) * GROUP, :]
                inner = state_ref[tile, own_rows, :]
                north, south = ((outer, inner), (inner, outer))[side]
                result = stencil(here, east, west, north, south, shares)
                extra = turned(field, zonal, meridional, coriolis_edge)
                if extra is not None:
                    result = result + extra
                place = MAIN + side * PAIRS + field * GROUP
                stepped_ref[tile, place : place + GROUP, :] = jnp.where(exists > 0.5, result, 0.0)
                stepped_ref[tile, own_rows, :] = stepped_ref[tile, own_rows, :] + given * here

    wanted = jnp.zeros((ROWS, COLS), jnp.int32)
    for row in range(ROWS):
        wanted = jnp.where(sub == row, filter_ref[first + row], wanted)
    wanted_main = jnp.concatenate([wanted] * PAIRS, axis=0) == 1
    wanted_above = filter_ref[jnp.minimum(first + ROWS, N_LAT * ROWS - 1)]
    wanted_below = filter_ref[jnp.maximum(first - 1, 0)]
    edge_row = lax.broadcasted_iota(jnp.int32, (EDGE_PAD, COLS), 0)
    wanted_edge = jnp.where(edge_row < PAIRS, wanted_above, wanted_below) == 1

    def polar_filter(rows, target):
        for tile in range(N_LON):
            high, low = halves(stepped_ref[tile, :rows, :])
            split_ref[:rows, tile * COLS : (tile + 1) * COLS] = high
            split_ref[rows : 2 * rows, tile * COLS : (tile + 1) * COLS] = low
        sums = jnp.dot(split_ref[: 2 * rows, :], analysis_ref[...], preferred_element_type=F32)
        sums = sums[:rows] + sums[rows:]
        sums = sums[:, :COLS] + sums[:, COLS:]
        high, low = halves(sums)
        both = jnp.concatenate(
            [jnp.concatenate([high, high], axis=1), jnp.concatenate([low, low], axis=1)], axis=0
        )
        for pair in range(N_LON // 2):
            smooth = jnp.dot(
                both,
                synthesis_ref[:, pair * 2 * COLS : (pair + 1) * 2 * COLS],
                preferred_element_type=F32,
            )
            smooth = smooth[:rows] + smooth[rows:]
            for side in range(2):
                tile = 2 * pair + side
                piece = smooth[:, side * COLS : (side + 1) * COLS]
                target[tile, :MAIN, :] = jnp.where(
                    wanted_main, piece[:MAIN], stepped_ref[tile, :MAIN, :]
                )
                if rows > MAIN:
                    target[tile, MAIN:rows, :] = jnp.where(
                        wanted_edge, piece[MAIN:], stepped_ref[tile, MAIN:rows, :]
                    )

    stepped_ref[:, MAIN + EDGE :, :] = jnp.zeros((N_LON, ALL - MAIN - EDGE, COLS), F32)
    for tile in range(N_LON):
        stepped_ref[tile, :MAIN, :] = inside_ref[tile]
    step_edge(0)
    step_edge(1)
    polar_filter(ALL, current_ref)
    step_main(
        current_ref,
        stepped_ref,
        lambda tile, pair: current_ref[tile, pl.ds(MAIN + pair, 1), :],
        lambda tile, pair: current_ref[tile, pl.ds(MAIN + PAIRS + pair, 1), :],
        metric,
        coriolis,
    )
    polar_filter(MAIN, out_ref)


def prepare_kernel(mixing_ref, map_ref, gain_ref, inverse_ref, order_ref):
    mix = mixing_ref[...]

    def level_step(level, above):
        inside = jnp.where((level == 0) | (level == LEVELS - 1), 1.0, 2.0)
        inverse = 1.0 / (1.0 + inside * mix - mix * above)
        gain = mix * inverse
        gain_ref[level] = gain
        inverse_ref[level] = inverse
        return gain

    lax.fori_loop(0, LEVELS, level_step, jnp.zeros_like(mix))

    target = map_ref[...] // COLUMNS
    before = lax.broadcasted_iota(jnp.int32, (COLS, 2 * COLS), 0)
    after = lax.broadcasted_iota(jnp.int32, (COLS, 2 * COLS), 1)
    counter = jnp.where((before < after) | (after >= COLS), 1.0, 0.0).astype(BF16)
    block = lax.broadcasted_iota(jnp.int32, (BLOCKS, COLS), 0)
    place = lax.broadcasted_iota(jnp.int32, (COLUMNS, COLS), 0)
    earlier = jnp.zeros((BLOCKS, COLS), F32)
    for row in range(ROWS):
        goal = target[row : row + 1, :]
        chosen = jnp.where(block == goal, 1.0, 0.0)
        counted = jnp.dot(chosen.astype(BF16), counter, preferred_element_type=F32)
        rank = jnp.sum(chosen * (counted[:, :COLS] + earlier), axis=0, keepdims=True)
        earlier = earlier + counted[:, COLS:]
        seat = goal * ROWS + rank.astype(jnp.int32)
        order_ref[:, row * COLS : (row + 1) * COLS] = jnp.where(place == seat, 1.0, 0.0).astype(BF16)


def physics_kernel(
    dyn_ref, mixing_ref, sun_ref, map_ref, gain_ref, inverse_ref, order_ref,
    out_ref, send_ref, heating_ref, table_ref,
):
    zero = jnp.zeros((ROWS, COLS), F32)

    def forward(group, carry):
        for inner in range(GROUP):
            level = group * GROUP + inner
            gain = gain_ref[level]
            inverse = inverse_ref[level]
            carry = tuple(
                dyn_ref[group, (field * GROUP + inner) * ROWS : (field * GROUP + inner + 1) * ROWS, :]
                * inverse
                + gain * carry[field]
                for field in range(FIELDS)
            )
            for field in range(FIELDS):
                out_ref[field, level] = carry[field]
        return carry

    lax.fori_loop(0, N_LON, forward, (zero,) * FIELDS)
    sun = RADIATE * sun_ref[...]

    def backward(step, carry):
        group = N_LON - 1 - step
        for inner in reversed(range(GROUP)):
            level = group * GROUP + inner
            gain = gain_ref[level]
            carry = tuple(out_ref[field, level] + gain * carry[field] for field in range(FIELDS))
            warmed = carry[2] + sun * carry[3]
            out_ref[0, level] = carry[0]
            out_ref[1, level] = carry[1]
            out_ref[2, level] = warmed
            out_ref[3, level] = carry[3]
            at = (2 * GROUP + inner) * ROWS
            heating_ref[pl.ds(pl.multiple_of(level * ROWS, ROWS), ROWS), :] = (
                warmed - dyn_ref[group, at : at + ROWS, :]
            )
        return carry

    lax.fori_loop(0, N_LON, backward, (zero,) * FIELDS)

    slots = (map_ref[...] % COLUMNS).astype(F32)
    top = lax.broadcasted_iota(jnp.int32, (COLS - LEVELS, COLS), 0) == 0
    for row in range(ROWS):
        body = heating_ref[pl.ds(row, LEVELS, stride=ROWS), :]
        tail = jnp.where(top, slots[row : row + 1, :], 0.0)
        high, low = halves(jnp.concatenate([body, tail], axis=0))
        table_ref[:COLS, row * COLS : (row + 1) * COLS] = high
        table_ref[COLS:, row * COLS : (row + 1) * COLS] = low
    sent = lax.dot_general(
        order_ref[...], table_ref[...], (((1,), (1,)), ((), ())), preferred_element_type=F32
    )
    send_ref[...] = sent[:, :COLS] + sent[:, COLS:]


def place_kernel(got_ref, out_ref):
    got = got_ref[...]
    slot = got[:, LEVELS : LEVELS + 1]
    column = lax.broadcasted_iota(jnp.int32, (COLUMNS, COLUMNS), 1).astype(F32)
    chosen = jnp.where(column == slot, 1.0, 0.0).astype(BF16)
    high, low = halves(got.T[:LEVELS])
    both = jnp.concatenate([high, low], axis=0)
    placed = jnp.dot(both, chosen, preferred_element_type=F32)
    out_ref[0] = placed[:LEVELS] + placed[LEVELS:]


def per_device(state, mixing, insolation, filter_rows, block_map):
    analysis, synthesis = (jnp.asarray(table) for table in fourier_tables())
    rows = jnp.asarray(row_tables())
    band = lax.axis_index("lat").astype(jnp.int32).reshape(1)

    state, band = lax.optimization_barrier((state, band))
    by_group = state.reshape(FIELDS, N_LON, GROUP, ROWS, COLS).transpose(1, 0, 2, 3, 4)
    circles = lax.all_to_all(
        by_group.reshape(N_LON, MAIN, COLS), "lon", split_axis=0, concat_axis=0, tiled=True
    )
    edge = ((N_LON, EDGE, COLS), F32)
    to_near, to_far = call(pack_kernel, "pack", (edge, edge), [], 4, band, circles, scalars=1)
    near = lax.ppermute(to_near, "lat", [(i, i ^ 1) for i in range(N_LAT)])
    far = lax.ppermute(
        to_far, "lat", [(i, ((i + 1) ^ 1) - 1) for i in range(1, N_LAT - 1)]
    )
    (inside,) = call(
        inside_kernel, "inside", (((N_LON, MAIN, COLS), F32),), [], 4, band, circles, rows,
        scalars=1, after=(to_near, to_far),
    )
    levels = ((LEVELS, ROWS, COLS), F32)
    gain, inverse, order = call(
        prepare_kernel, "prepare", (levels, levels, ((COLUMNS, COLUMNS), BF16)), [], 4,
        mixing, block_map,
        after=(to_near,),
    )
    (dyn,) = call(
        dynamics_kernel,
        "dynamics",
        (((N_LON, MAIN, COLS), F32),),
        [
            pltpu.VMEM((N_LON, EDGE, COLS), F32),
            pltpu.VMEM((N_LON, EDGE, COLS), F32),
            pltpu.VMEM((N_LON, ALL, COLS), F32),
            pltpu.VMEM((N_LON, ALL, COLS), F32),
            pltpu.VMEM((2 * ALL, CIRCLE), BF16),
        ],
        16,
        band, filter_rows, circles, inside, near, far, rows, analysis, synthesis,
        scalars=2,
        after=(gain,),
    )
    columns = lax.all_to_all(dyn, "lon", split_axis=0, concat_axis=0, tiled=True)
    new_state, sent = call(
        physics_kernel,
        "physics",
        (((FIELDS, LEVELS, ROWS, COLS), F32), ((COLUMNS, COLS), F32)),
        [pltpu.VMEM((LEVELS * ROWS, COLS), F32), pltpu.VMEM((2 * COLS, COLUMNS), BF16)],
        12,
        columns, mixing, insolation, block_map, gain, inverse, order,
        stored=(),
    )
    got = lax.all_to_all(
        sent.reshape(BLOCKS, ROWS, COLS), ("lat", "lon"), split_axis=0, concat_axis=0, tiled=True
    )
    (block_heating,) = call(
        place_kernel, "place", (((1, LEVELS, COLUMNS), F32),), [], 8, got.reshape(COLUMNS, COLS),
        stored=(0,),
    )
    return new_state, block_heating


def solution(mesh):
    in_specs = (P(None, None, "lat", "lon"), P("lat", "lon"), P("lat", "lon"), P(), P("lat", "lon"))
    out_specs = (P(None, None, "lat", "lon"), P(("lat", "lon"), None, None))
    return jax.shard_map(
        per_device, mesh=mesh, in_specs=in_specs, out_specs=out_specs, check_vma=False
    )
```

```python
import math

import jax
import jax.numpy as jnp
import numpy as np
from jax import lax
from jax.experimental import pallas as pl
from jax.experimental.pallas import tpu as pltpu
from jax.sharding import PartitionSpec as P

KEEP = 64
ADVECT = 0.1
DIFFUSE = 0.1
ROTATE = 0.2
RADIATE = 0.5
FLOOR = 0.25

FIELDS = 4
LEVELS = 80
ROWS = 8
COLS = 128
N_LAT = 8
N_LON = 16
GROUP = LEVELS // N_LON
PAIRS = FIELDS * GROUP
MAIN = PAIRS * ROWS
EDGE = 2 * PAIRS
COLUMNS = ROWS * COLS
BLOCKS = N_LAT * N_LON
CIRCLE = COLS * N_LON

F32 = jnp.float32
BF16 = jnp.bfloat16
VMEM = pl.BlockSpec(memory_space=pltpu.VMEM)
HBM = pl.BlockSpec(memory_space=pltpu.HBM)
ANY = pl.BlockSpec(memory_space=pl.ANY)
SMEM = pl.BlockSpec(memory_space=pltpu.SMEM)


def call(kernel, name, out_shapes, scratch, megabytes, *args, scalars=0, stored=(), after=(), left=(), taken=()):
    def body(*refs):
        kernel(*refs[: len(args)], *refs[len(args) + len(after) :])

    placed = args[:scalars] + tuple(
        pltpu.with_memory_space_constraint(arg, pltpu.HBM if index in taken else pltpu.VMEM)
        for index, arg in enumerate(args[scalars:])
    )
    return pl.pallas_call(
        body,
        out_shape=tuple(
            jax.ShapeDtypeStruct(shape, kind) if index in stored + left else pltpu.VMEM(shape, kind)
            for index, (shape, kind) in enumerate(out_shapes)
        ),
        in_specs=[SMEM] * scalars
        + [HBM if index in taken else VMEM for index in range(len(args) - scalars)]
        + [ANY] * len(after),
        out_specs=tuple(ANY if index in left else VMEM for index in range(len(out_shapes))),
        scratch_shapes=scratch,
        compiler_params=pltpu.CompilerParams(vmem_limit_bytes=megabytes << 20),
        name=name,
    )(*placed, *after)


def halves(values):
    high = values.astype(BF16)
    low = (values - high.astype(F32)).astype(BF16)
    return high, low


def fourier_tables():
    waves = np.arange(KEEP)
    phase = 2.0 * math.pi / CIRCLE * (np.outer(np.arange(CIRCLE), waves) % CIRCLE)
    analysis = np.concatenate([np.cos(phase), np.sin(phase)], axis=1)
    weights = np.where(waves == 0, 1.0, 2.0)[:, None] / CIRCLE
    synthesis = np.concatenate([weights * np.cos(phase.T), weights * np.sin(phase.T)], axis=0)

    def split(table, axis):
        high = table.astype(BF16)
        low = (table - high.astype(np.float64)).astype(BF16)
        return np.concatenate([high, low], axis=axis)

    return split(analysis, 1), split(synthesis, 0)


def row_tables():
    total = N_LAT * ROWS
    table = np.zeros((N_LAT, 9, ROWS, COLS), np.float32)
    rows = np.arange(-1, total + 1)
    latitude = (rows + 0.5) * (math.pi / total) - 0.5 * math.pi
    metric = 1.0 / np.maximum(np.cos(latitude), FLOOR)
    coriolis = np.sin(latitude)
    for band in range(N_LAT):
        first = band * ROWS
        table[band, 0] = metric[first + 1 : first + 1 + ROWS, None]
        table[band, 1] = coriolis[first + 1 : first + 1 + ROWS, None]
        table[band, 2] = metric[first + 1 + ROWS]
        table[band, 3] = coriolis[first + 1 + ROWS]
        table[band, 4] = float(band < N_LAT - 1)
        table[band, 5] = metric[first]
        table[band, 6] = coriolis[first]
        table[band, 7] = float(band > 0)
        table[band, 8] = float(band % 2 == 0)
    return table


def gather_kernel(
    band_ref, state_ref, rows_ref, filter_ref,
    out_ref, band_rows_ref, wanted_ref, filter_scratch, done_ref,
):
    band = band_ref[0]
    copies = [
        pltpu.make_async_copy(
            state_ref.at[field],
            out_ref.at[:, field * GROUP * ROWS : (field + 1) * GROUP * ROWS, :],
            done_ref.at[field],
        )
        for field in range(FIELDS)
    ]
    copies.append(pltpu.make_async_copy(rows_ref.at[band], band_rows_ref, done_ref.at[FIELDS]))
    fetch = pltpu.make_async_copy(filter_ref, filter_scratch, done_ref.at[FIELDS + 1])
    fetch.start()
    for copy in copies:
        copy.start()
    fetch.wait()
    first = band * ROWS
    sub = lax.broadcasted_iota(jnp.int32, (ROWS, COLS), 0)
    wanted = jnp.zeros((ROWS, COLS), jnp.int32)
    for row in range(ROWS):
        wanted = jnp.where(sub == row, filter_scratch[first + row], wanted)
    for pair in range(PAIRS):
        wanted_ref[pair * ROWS : (pair + 1) * ROWS, :] = wanted
    beyond = (
        jnp.minimum(first + ROWS, N_LAT * ROWS - 1), jnp.maximum(first - 1, 0),
        first + ROWS - 1, first,
    )
    for place, row in enumerate(beyond):
        wanted_ref[MAIN + place * PAIRS : MAIN + (place + 1) * PAIRS, :] = jnp.full(
            (PAIRS, COLS), filter_scratch[row], jnp.int32
        )
    for copy in copies:
        copy.wait()


def pack_kernel(band_ref, state_ref, near_ref, far_ref):
    odd = band_ref[0] % 2
    near_row = (ROWS - 2) * (1 - odd)
    far_row = (ROWS - 2) * odd
    for tile in range(N_LON):
        for ref, row in ((near_ref, near_row), (far_ref, far_row)):
            for place in range(2):
                ref[tile, pl.ds(place * PAIRS, PAIRS), :] = state_ref[
                    tile, pl.ds(row + place, PAIRS, stride=ROWS), :
                ]


def weights(zonal, meridional, metric):
    along = ADVECT * (zonal * metric)
    across = ADVECT * meridional
    return DIFFUSE - along, DIFFUSE + along, DIFFUSE - across, DIFFUSE + across


def stencil(center, east, west, north, south, shares):
    to_east, to_west, to_north, to_south = shares
    return (
        (1.0 - 4.0 * DIFFUSE) * center
        + (to_east * east + to_west * west)
        + (to_north * north + to_south * south)
    )


def turned(field, zonal, meridional, coriolis):
    if field == 0:
        return ROTATE * coriolis * meridional
    if field == 1:
        return -ROTATE * coriolis * zonal
    return None


def neighbours(load, lanes):
    kept = {}

    def rolled(tile, shift):
        tile = tile % N_LON
        if (tile, shift) not in kept:
            kept[tile, shift] = pltpu.roll(load(tile), shift, 1)
        return kept[tile, shift]

    def beside(tile):
        east = jnp.where(lanes == COLS - 1, rolled(tile + 1, COLS - 1), rolled(tile, COLS - 1))
        west = jnp.where(lanes == 0, rolled(tile - 1, 1), rolled(tile, 1))
        return load(tile), east, west

    return beside


def step_main(source, target, north_of, south_of, metric, coriolis):
    lane = lax.broadcasted_iota(jnp.int32, (ROWS, COLS), 1)
    sub = lax.broadcasted_iota(jnp.int32, (ROWS, COLS), 0)

    def level_step(level, carry):
        def at(field):
            return pl.ds(pl.multiple_of((field * GROUP + level) * ROWS, ROWS), ROWS)

        def reader(field):
            kept = {}

            def load(tile):
                if tile not in kept:
                    kept[tile] = source[tile, at(field), :]
                return kept[tile]

            return load

        beside = [neighbours(reader(field), lane) for field in range(FIELDS)]
        for tile in range(N_LON):
            zonal = source[tile, at(0), :]
            meridional = source[tile, at(1), :]
            shares = weights(zonal, meridional, metric)
            for field in range(FIELDS):
                pair = field * GROUP + level
                here, east, west = beside[field](tile)
                north = jnp.where(
                    sub == ROWS - 1, north_of(tile, pair), pltpu.roll(here, ROWS - 1, 0)
                )
                south = jnp.where(sub == 0, south_of(tile, pair), pltpu.roll(here, 1, 0))
                result = stencil(here, east, west, north, south, shares)
                extra = turned(field, zonal, meridional, coriolis)
                if extra is not None:
                    result = result + extra
                target[tile, at(field), :] = result
        return carry

    lax.fori_loop(0, GROUP, level_step, 0)


def fourier_sums(load, analysis_ref):
    high, low = zip(*(halves(load(tile)) for tile in range(N_LON)))
    both = jnp.concatenate(
        [jnp.concatenate(high, axis=1), jnp.concatenate(low, axis=1)], axis=0
    )
    sums = jnp.dot(both, analysis_ref[...], preferred_element_type=F32)
    rows = sums.shape[0] // 2
    sums = sums[:rows] + sums[rows:]
    return sums[:, :COLS] + sums[:, COLS:]


def smooth_rows(sums, synthesis_ref):
    rows = sums.shape[0]
    high, low = halves(sums)
    both = jnp.concatenate(
        [jnp.concatenate([high, high], axis=1), jnp.concatenate([low, low], axis=1)], axis=0
    )
    for pair in range(N_LON // 2):
        smooth = jnp.dot(
            both,
            synthesis_ref[:, pair * 2 * COLS : (pair + 1) * 2 * COLS],
            preferred_element_type=F32,
        )
        smooth = smooth[:rows] + smooth[rows:]
        yield 2 * pair, smooth[:, :COLS]
        yield 2 * pair + 1, smooth[:, COLS:]


def filter_main(stepped_ref, target_ref, wanted_ref, analysis_ref, synthesis_ref):
    sums = fourier_sums(lambda tile: stepped_ref[tile], analysis_ref)
    for tile, smooth in smooth_rows(sums, synthesis_ref):
        target_ref[tile] = jnp.where(wanted_ref[:MAIN, :] == 1, smooth, stepped_ref[tile])


def inside_kernel(
    state_ref, rows_ref, wanted_ref, analysis_ref, synthesis_ref, out_ref, stepped_ref
):
    step_main(
        state_ref, stepped_ref, lambda tile, pair: 0.0, lambda tile, pair: 0.0,
        rows_ref[0], rows_ref[1],
    )
    filter_main(stepped_ref, out_ref, wanted_ref, analysis_ref, synthesis_ref)


def dynamics_kernel(
    state_ref, inside_ref, near_ref, far_ref, rows_ref, wanted_ref, analysis_ref,
    synthesis_ref, out_ref, north_ref, south_ref, stepped_ref, current_ref, edge_ref,
):
    lane_edge = lax.broadcasted_iota(jnp.int32, (GROUP, COLS), 1)
    metric = rows_ref[0]
    coriolis = rows_ref[1]

    even = jnp.concatenate([rows_ref[8]] * (EDGE // ROWS), axis=0) > 0.5
    for tile in range(N_LON):
        near_rows = near_ref[tile]
        far_rows = far_ref[tile]
        north_ref[tile] = jnp.where(even, near_rows, far_rows)
        south_ref[tile] = jnp.where(even, far_rows, near_rows)

    def step_edge(side):
        base = 2 + 3 * side
        metric_edge = rows_ref[base][:GROUP]
        coriolis_edge = rows_ref[base + 1][:GROUP]
        exists = rows_ref[base + 2][:GROUP]
        halo = (north_ref, south_ref)[side]
        near = (0, PAIRS)[side]
        far = (PAIRS, 0)[side]
        own = (ROWS - 1, 0)[side]
        beside = [
            neighbours(
                lambda t, at=near + field * GROUP: halo[t, at : at + GROUP, :], lane_edge
            )
            for field in range(FIELDS)
        ]
        for tile in range(N_LON):
            zonal = halo[tile, near : near + GROUP, :]
            meridional = halo[tile, near + GROUP : near + 2 * GROUP, :]
            shares = weights(zonal, meridional, metric_edge)
            own_wind = state_ref[tile, pl.ds(GROUP * ROWS + own, GROUP, stride=ROWS), :]
            given = DIFFUSE + (-ADVECT, ADVECT)[side] * own_wind
            for field in range(FIELDS):
                own_rows = pl.ds(field * GROUP * ROWS + own, GROUP, stride=ROWS)
                here, east, west = beside[field](tile)
                outer = halo[tile, far + field * GROUP : far + (field + 1) * GROUP, :]
                inner = state_ref[tile, own_rows, :]
                north, south = ((outer, inner), (inner, outer))[side]
                result = stencil(here, east, west, north, south, shares)
                extra = turned(field, zonal, meridional, coriolis_edge)
                if extra is not None:
                    result = result + extra
                place = MAIN + side * PAIRS + field * GROUP
                result = jnp.where(exists > 0.5, result, 0.0)
                place = side * PAIRS + field * GROUP
                edge_ref[tile, place : place + GROUP, :] = result
                place = EDGE + place
                edge_ref[tile, place : place + GROUP, :] = given * here

    step_edge(0)
    step_edge(1)
    sums = fourier_sums(lambda tile: edge_ref[tile], analysis_ref)
    for tile, smooth in smooth_rows(sums, synthesis_ref):
        edge = jnp.where(wanted_ref[MAIN:, :] == 1, smooth, edge_ref[tile])
        current_ref[tile, :MAIN, :] = inside_ref[tile]
        current_ref[tile, MAIN:, :] = edge[:EDGE]
        for side, own in enumerate((ROWS - 1, 0)):
            rows = pl.ds(own, PAIRS, stride=ROWS)
            place = EDGE + side * PAIRS
            current_ref[tile, rows, :] = (
                current_ref[tile, rows, :] + edge[place : place + PAIRS]
            )
    step_main(
        current_ref,
        stepped_ref,
        lambda tile, pair: current_ref[tile, pl.ds(MAIN + pair, 1), :],
        lambda tile, pair: current_ref[tile, pl.ds(MAIN + PAIRS + pair, 1), :],
        metric,
        coriolis,
    )
    filter_main(stepped_ref, out_ref, wanted_ref, analysis_ref, synthesis_ref)


def prepare_kernel(mixing_ref, map_ref, gain_ref, inverse_ref, order_ref):
    mix = mixing_ref[...]
    gain = jnp.zeros_like(mix)
    for level in range(LEVELS):
        inside = 1.0 if level in (0, LEVELS - 1) else 2.0
        inverse = 1.0 / (1.0 + inside * mix - mix * gain)
        gain = mix * inverse
        gain_ref[level] = gain
        inverse_ref[level] = inverse

    target = map_ref[...] // COLUMNS
    before = lax.broadcasted_iota(jnp.int32, (COLS, 2 * COLS), 0)
    after = lax.broadcasted_iota(jnp.int32, (COLS, 2 * COLS), 1)
    counter = jnp.where((before < after) | (after >= COLS), 1.0, 0.0).astype(BF16)
    block = lax.broadcasted_iota(jnp.int32, (BLOCKS, COLS), 0)
    sub = lax.broadcasted_iota(jnp.int32, (2 * ROWS, COLS), 0)
    earlier = jnp.zeros((BLOCKS, COLS), F32)
    one = jnp.ones((2 * ROWS, COLS), BF16)
    zero = jnp.zeros((2 * ROWS, COLS), BF16)
    for row in range(ROWS):
        goal = target[row : row + 1, :]
        chosen = jnp.where(block == goal, 1.0, 0.0)
        counted = jnp.dot(chosen.astype(BF16), counter, preferred_element_type=F32)
        rank = jnp.sum(chosen * (counted[:, :COLS] + earlier), axis=0, keepdims=True)
        earlier = earlier + counted[:, COLS:]
        seat = rank.astype(jnp.int32)
        pair = jnp.where(
            sub == seat, goal, jnp.where(sub == seat + ROWS, goal - 1, -1)
        ).astype(F32).astype(BF16)
        for even in range(0, BLOCKS, 2):
            order_ref[even * ROWS : (even + 2) * ROWS, row * COLS : (row + 1) * COLS] = jnp.where(
                pair == jnp.asarray(even, BF16), one, zero
            )


def physics_kernel(
    dyn_ref, mixing_ref, sun_ref, map_ref, gain_ref, inverse_ref, order_ref,
    stored_ref, send_ref, out_ref, heating_ref, table_ref, done_ref,
):
    zero = jnp.zeros((ROWS, COLS), F32)

    def forward(group, carry):
        for inner in range(GROUP):
            level = group * GROUP + inner
            gain = gain_ref[level]
            inverse = inverse_ref[level]
            carry = tuple(
                dyn_ref[group, (field * GROUP + inner) * ROWS : (field * GROUP + inner + 1) * ROWS, :]
                * inverse
                + gain * carry[field]
                for field in range(FIELDS)
            )
            for field in range(FIELDS):
                out_ref[field, level] = carry[field]
        return carry

    lax.fori_loop(0, N_LON, forward, (zero,) * FIELDS)
    sun = RADIATE * sun_ref[...]

    def backward(step, carry):
        group = N_LON - 1 - step
        for inner in reversed(range(GROUP)):
            level = group * GROUP + inner
            gain = gain_ref[level]
            carry = tuple(out_ref[field, level] + gain * carry[field] for field in range(FIELDS))
            warmed = carry[2] + sun * carry[3]
            out_ref[0, level] = carry[0]
            out_ref[1, level] = carry[1]
            out_ref[2, level] = warmed
            out_ref[3, level] = carry[3]
            at = (2 * GROUP + inner) * ROWS
            heating_ref[pl.ds(pl.multiple_of(level * ROWS, ROWS), ROWS), :] = (
                warmed - dyn_ref[group, at : at + ROWS, :]
            )
        return carry

    lax.fori_loop(0, N_LON, backward, (zero,) * FIELDS)

    store = pltpu.make_async_copy(out_ref, stored_ref, done_ref)
    store.start()
    slots = (map_ref[...] % COLUMNS).astype(F32)
    top = lax.broadcasted_iota(jnp.int32, (COLS - LEVELS, COLS), 0) == 0
    for row in range(ROWS):
        body = heating_ref[pl.ds(row, LEVELS, stride=ROWS), :]
        tail = jnp.where(top, slots[row : row + 1, :], 0.0)
        high, low = halves(jnp.concatenate([body, tail], axis=0))
        table_ref[:COLS, row * COLS : (row + 1) * COLS] = high
        table_ref[COLS:, row * COLS : (row + 1) * COLS] = low
    sent = lax.dot_general(
        order_ref[...], table_ref[...], (((1,), (1,)), ((), ())), preferred_element_type=F32
    )
    send_ref[...] = sent[:, :COLS] + sent[:, COLS:]
    store.wait()


def place_kernel(got_ref, out_ref):
    got = got_ref[...]
    slot = got[:, LEVELS : LEVELS + 1]
    column = lax.broadcasted_iota(jnp.int32, (COLUMNS, COLUMNS), 1).astype(F32)
    chosen = jnp.where(column == slot, 1.0, 0.0).astype(BF16)
    high, low = halves(got.T[:LEVELS])
    both = jnp.concatenate([high, low], axis=0)
    placed = jnp.dot(both, chosen, preferred_element_type=F32)
    out_ref[0] = placed[:LEVELS] + placed[LEVELS:]


def per_device(state, mixing, insolation, filter_rows, block_map):
    analysis, synthesis = (jnp.asarray(table) for table in fourier_tables())
    rows = jnp.asarray(row_tables())
    band = lax.axis_index("lat").astype(jnp.int32).reshape(1)

    state, band = lax.optimization_barrier((state, band))
    by_group, band_rows, wanted = call(
        gather_kernel, "gather",
        (
            ((N_LON, MAIN, COLS), F32),
            (rows.shape[1:], F32),
            ((MAIN + 2 * EDGE, COLS), jnp.int32),
        ),
        [pltpu.SMEM((N_LAT * ROWS,), jnp.int32), pltpu.SemaphoreType.DMA((FIELDS + 2,))], 1,
        band, state.reshape(FIELDS, N_LON, GROUP * ROWS, COLS), rows, filter_rows,
        scalars=1, taken=(0, 1, 2),
    )
    circles = lax.all_to_all(by_group, "lon", split_axis=0, concat_axis=0, tiled=True)
    edge = ((N_LON, EDGE, COLS), F32)
    to_near, to_far = call(pack_kernel, "pack", (edge, edge), [], 4, band, circles, scalars=1)
    near = lax.ppermute(to_near, "lat", [(i, i ^ 1) for i in range(N_LAT)])
    far = lax.ppermute(
        to_far, "lat", [(i, ((i + 1) ^ 1) - 1) for i in range(1, N_LAT - 1)]
    )
    (inside,) = call(
        inside_kernel, "inside", (((N_LON, MAIN, COLS), F32),),
        [pltpu.VMEM((N_LON, MAIN, COLS), F32)], 8,
        circles, band_rows, wanted, analysis, synthesis,
        after=(to_near, to_far),
    )
    levels = ((LEVELS, ROWS, COLS), F32)
    gain, inverse, order = call(
        prepare_kernel, "prepare", (levels, levels, ((COLUMNS, COLUMNS), BF16)), [], 4,
        mixing, block_map,
        after=(to_near,),
    )
    (dyn,) = call(
        dynamics_kernel,
        "dynamics",
        (((N_LON, MAIN, COLS), F32),),
        [
            pltpu.VMEM((N_LON, EDGE, COLS), F32),
            pltpu.VMEM((N_LON, EDGE, COLS), F32),
            pltpu.VMEM((N_LON, MAIN, COLS), F32),
            pltpu.VMEM((N_LON, MAIN + EDGE, COLS), F32),
            pltpu.VMEM((N_LON, 2 * EDGE, COLS), F32),
        ],
        16,
        circles, inside, near, far, band_rows, wanted, analysis, synthesis,
        after=(gain,),
    )
    columns = lax.all_to_all(dyn, "lon", split_axis=0, concat_axis=0, tiled=True)
    new_state, sent = call(
        physics_kernel,
        "physics",
        (((FIELDS, LEVELS, ROWS, COLS), F32), ((COLUMNS, COLS), F32)),
        [
            pltpu.VMEM((FIELDS, LEVELS, ROWS, COLS), F32),
            pltpu.VMEM((LEVELS * ROWS, COLS), F32),
            pltpu.VMEM((2 * COLS, COLUMNS), BF16),
            pltpu.SemaphoreType.DMA(()),
        ],
        12,
        columns, mixing, insolation, block_map, gain, inverse, order,
        left=(0,),
    )
    got = lax.all_to_all(
        sent.reshape(BLOCKS, ROWS, COLS), ("lat", "lon"), split_axis=0, concat_axis=0, tiled=True
    )
    (block_heating,) = call(
        place_kernel, "place", (((1, LEVELS, COLUMNS), F32),), [], 8, got.reshape(COLUMNS, COLS),
        stored=(0,),
    )
    return new_state, block_heating


def solution(mesh):
    in_specs = (P(None, None, "lat", "lon"), P("lat", "lon"), P("lat", "lon"), P(), P("lat", "lon"))
    out_specs = (P(None, None, "lat", "lon"), P(("lat", "lon"), None, None))
    return jax.shard_map(
        per_device, mesh=mesh, in_specs=in_specs, out_specs=out_specs, check_vma=False
    )
```

```python
import math

import jax
import jax.numpy as jnp
import numpy as np
from jax import lax
from jax.experimental import pallas as pl
from jax.experimental.pallas import tpu as pltpu
from jax.sharding import PartitionSpec as P

KEEP = 64
ADVECT = 0.1
DIFFUSE = 0.1
ROTATE = 0.2
RADIATE = 0.5
FLOOR = 0.25

FIELDS = 4
LEVELS = 80
ROWS = 8
COLS = 128
N_LAT = 8
N_LON = 16
GROUP = LEVELS // N_LON
PAIRS = FIELDS * GROUP
MAIN = PAIRS * ROWS
EDGE = 2 * PAIRS
COLUMNS = ROWS * COLS
BLOCKS = N_LAT * N_LON
CIRCLE = COLS * N_LON

F32 = jnp.float32
BF16 = jnp.bfloat16
VMEM = pl.BlockSpec(memory_space=pltpu.VMEM)
HBM = pl.BlockSpec(memory_space=pltpu.HBM)
ANY = pl.BlockSpec(memory_space=pl.ANY)
SMEM = pl.BlockSpec(memory_space=pltpu.SMEM)


def call(kernel, name, out_shapes, scratch, megabytes, *args, scalars=0, stored=(), after=(), left=(), taken=()):
    def body(*refs):
        kernel(*refs[: len(args)], *refs[len(args) + len(after) :])

    placed = args[:scalars] + tuple(
        pltpu.with_memory_space_constraint(arg, pltpu.HBM if index in taken else pltpu.VMEM)
        for index, arg in enumerate(args[scalars:])
    )
    return pl.pallas_call(
        body,
        out_shape=tuple(
            jax.ShapeDtypeStruct(shape, kind) if index in stored + left else pltpu.VMEM(shape, kind)
            for index, (shape, kind) in enumerate(out_shapes)
        ),
        in_specs=[SMEM] * scalars
        + [HBM if index in taken else VMEM for index in range(len(args) - scalars)]
        + [ANY] * len(after),
        out_specs=tuple(ANY if index in left else VMEM for index in range(len(out_shapes))),
        scratch_shapes=scratch,
        compiler_params=pltpu.CompilerParams(vmem_limit_bytes=megabytes << 20),
        name=name,
    )(*placed, *after)


def halves(values):
    high = values.astype(BF16)
    low = (values - high.astype(F32)).astype(BF16)
    return high, low


def fourier_tables():
    waves = np.arange(KEEP)
    phase = 2.0 * math.pi / CIRCLE * (np.outer(np.arange(CIRCLE), waves) % CIRCLE)
    analysis = np.concatenate([np.cos(phase), np.sin(phase)], axis=1)
    weights = np.where(waves == 0, 1.0, 2.0)[:, None] / CIRCLE
    synthesis = np.concatenate([weights * np.cos(phase.T), weights * np.sin(phase.T)], axis=0)

    def split(table, axis):
        high = table.astype(BF16)
        low = (table - high.astype(np.float64)).astype(BF16)
        return np.concatenate([high, low], axis=axis)

    return split(analysis, 1), split(synthesis, 0)


def row_tables():
    total = N_LAT * ROWS
    table = np.zeros((N_LAT, 9, ROWS, COLS), np.float32)
    rows = np.arange(-1, total + 1)
    latitude = (rows + 0.5) * (math.pi / total) - 0.5 * math.pi
    metric = 1.0 / np.maximum(np.cos(latitude), FLOOR)
    coriolis = np.sin(latitude)
    for band in range(N_LAT):
        first = band * ROWS
        table[band, 0] = metric[first + 1 : first + 1 + ROWS, None]
        table[band, 1] = coriolis[first + 1 : first + 1 + ROWS, None]
        table[band, 2] = metric[first + 1 + ROWS]
        table[band, 3] = coriolis[first + 1 + ROWS]
        table[band, 4] = float(band < N_LAT - 1)
        table[band, 5] = metric[first]
        table[band, 6] = coriolis[first]
        table[band, 7] = float(band > 0)
        table[band, 8] = float(band % 2 == 0)
    return table


def gather_kernel(
    band_ref, state_ref, rows_ref, filter_ref,
    out_ref, band_rows_ref, wanted_ref, filter_scratch, done_ref,
):
    band = band_ref[0]
    copies = [
        pltpu.make_async_copy(
            state_ref.at[field],
            out_ref.at[:, field * GROUP * ROWS : (field + 1) * GROUP * ROWS, :],
            done_ref.at[field],
        )
        for field in range(FIELDS)
    ]
    copies.append(pltpu.make_async_copy(rows_ref.at[band], band_rows_ref, done_ref.at[FIELDS]))
    fetch = pltpu.make_async_copy(filter_ref, filter_scratch, done_ref.at[FIELDS + 1])
    fetch.start()
    for copy in copies:
        copy.start()
    fetch.wait()
    first = band * ROWS
    sub = lax.broadcasted_iota(jnp.int32, (ROWS, COLS), 0)
    wanted = jnp.zeros((ROWS, COLS), jnp.int32)
    for row in range(ROWS):
        wanted = jnp.where(sub == row, filter_scratch[first + row], wanted)
    for pair in range(PAIRS):
        wanted_ref[pair * ROWS : (pair + 1) * ROWS, :] = wanted
    beyond = (
        jnp.minimum(first + ROWS, N_LAT * ROWS - 1), jnp.maximum(first - 1, 0),
        first + ROWS - 1, first,
    )
    for place, row in enumerate(beyond):
        wanted_ref[MAIN + place * PAIRS : MAIN + (place + 1) * PAIRS, :] = jnp.full(
            (PAIRS, COLS), filter_scratch[row], jnp.int32
        )
    for copy in copies:
        copy.wait()


def pack_kernel(band_ref, state_ref, near_ref, far_ref):
    odd = band_ref[0] % 2
    near_row = (ROWS - 2) * (1 - odd)
    far_row = (ROWS - 2) * odd
    for tile in range(N_LON):
        for ref, row in ((near_ref, near_row), (far_ref, far_row)):
            for place in range(2):
                ref[tile, pl.ds(place * PAIRS, PAIRS), :] = state_ref[
                    tile, pl.ds(row + place, PAIRS, stride=ROWS), :
                ]


def weights(zonal, meridional, metric):
    along = ADVECT * (zonal * metric)
    across = ADVECT * meridional
    return DIFFUSE - along, DIFFUSE + along, DIFFUSE - across, DIFFUSE + across


def stencil(center, east, west, north, south, shares):
    to_east, to_west, to_north, to_south = shares
    return (
        (1.0 - 4.0 * DIFFUSE) * center
        + (to_east * east + to_west * west)
        + (to_north * north + to_south * south)
    )


def turned(field, zonal, meridional, coriolis):
    if field == 0:
        return ROTATE * coriolis * meridional
    if field == 1:
        return -ROTATE * coriolis * zonal
    return None


def neighbours(load, lanes):
    kept = {}

    def rolled(tile, shift):
        tile = tile % N_LON
        if (tile, shift) not in kept:
            kept[tile, shift] = pltpu.roll(load(tile), shift, 1)
        return kept[tile, shift]

    def beside(tile):
        east = jnp.where(lanes == COLS - 1, rolled(tile + 1, COLS - 1), rolled(tile, COLS - 1))
        west = jnp.where(lanes == 0, rolled(tile - 1, 1), rolled(tile, 1))
        return load(tile), east, west

    return beside


def step_main(source, target, north_of, south_of, metric, coriolis):
    lane = lax.broadcasted_iota(jnp.int32, (ROWS, COLS), 1)
    sub = lax.broadcasted_iota(jnp.int32, (ROWS, COLS), 0)

    def level_step(level, carry):
        def at(field):
            return pl.ds(pl.multiple_of((field * GROUP + level) * ROWS, ROWS), ROWS)

        def reader(field):
            kept = {}

            def load(tile):
                if tile not in kept:
                    kept[tile] = source[tile, at(field), :]
                return kept[tile]

            return load

        beside = [neighbours(reader(field), lane) for field in range(FIELDS)]
        for tile in range(N_LON):
            zonal = source[tile, at(0), :]
            meridional = source[tile, at(1), :]
            shares = weights(zonal, meridional, metric)
            for field in range(FIELDS):
                pair = field * GROUP + level
                here, east, west = beside[field](tile)
                north = jnp.where(
                    sub == ROWS - 1, north_of(tile, pair), pltpu.roll(here, ROWS - 1, 0)
                )
                south = jnp.where(sub == 0, south_of(tile, pair), pltpu.roll(here, 1, 0))
                result = stencil(here, east, west, north, south, shares)
                extra = turned(field, zonal, meridional, coriolis)
                if extra is not None:
                    result = result + extra
                target[tile, at(field), :] = result
        return carry

    lax.fori_loop(0, GROUP, level_step, 0)


def fourier_sums(load, analysis_ref):
    high, low = zip(*(halves(load(tile)) for tile in range(N_LON)))
    both = jnp.concatenate(
        [jnp.concatenate(high, axis=1), jnp.concatenate(low, axis=1)], axis=0
    )
    sums = jnp.dot(both, analysis_ref[...], preferred_element_type=F32)
    rows = sums.shape[0] // 2
    sums = sums[:rows] + sums[rows:]
    return sums[:, :COLS] + sums[:, COLS:]


def smooth_rows(band, sums, both_ref, synthesis_ref, emit):
    rows = sums.shape[0]
    high, low = halves(sums)
    both_ref[...] = jnp.concatenate(
        [jnp.concatenate([high, high], axis=1), jnp.concatenate([low, low], axis=1)], axis=0
    )

    @pl.when(band >= 0)
    def inverse():
        for pair in range(N_LON // 2):
            smooth = jnp.dot(
                both_ref[...],
                synthesis_ref[:, pair * 2 * COLS : (pair + 1) * 2 * COLS],
                preferred_element_type=F32,
            )
            smooth = smooth[:rows] + smooth[rows:]
            emit(2 * pair, smooth[:, :COLS])
            emit(2 * pair + 1, smooth[:, COLS:])


def filter_main(band, stepped_ref, target_ref, wanted_ref, analysis_ref, synthesis_ref, both_ref):
    sums = fourier_sums(lambda tile: stepped_ref[tile], analysis_ref)

    def emit(tile, smooth):
        target_ref[tile] = jnp.where(wanted_ref[:MAIN, :] == 1, smooth, stepped_ref[tile])

    smooth_rows(band, sums, both_ref, synthesis_ref, emit)


def inside_kernel(
    band_ref, state_ref, rows_ref, wanted_ref, analysis_ref, synthesis_ref,
    out_ref, stepped_ref, both_ref,
):
    step_main(
        state_ref, stepped_ref, lambda tile, pair: 0.0, lambda tile, pair: 0.0,
        rows_ref[0], rows_ref[1],
    )
    filter_main(band_ref[0], stepped_ref, out_ref, wanted_ref, analysis_ref, synthesis_ref, both_ref)


def dynamics_kernel(
    band_ref, state_ref, inside_ref, near_ref, far_ref, rows_ref, wanted_ref, analysis_ref,
    synthesis_ref, out_ref, north_ref, south_ref, stepped_ref, current_ref, edge_ref,
    both_edge_ref, both_ref,
):
    lane_edge = lax.broadcasted_iota(jnp.int32, (GROUP, COLS), 1)
    metric = rows_ref[0]
    coriolis = rows_ref[1]

    even = jnp.concatenate([rows_ref[8]] * (EDGE // ROWS), axis=0) > 0.5
    for tile in range(N_LON):
        near_rows = near_ref[tile]
        far_rows = far_ref[tile]
        north_ref[tile] = jnp.where(even, near_rows, far_rows)
        south_ref[tile] = jnp.where(even, far_rows, near_rows)

    def step_edge(side):
        base = 2 + 3 * side
        metric_edge = rows_ref[base][:GROUP]
        coriolis_edge = rows_ref[base + 1][:GROUP]
        exists = rows_ref[base + 2][:GROUP]
        halo = (north_ref, south_ref)[side]
        near = (0, PAIRS)[side]
        far = (PAIRS, 0)[side]
        own = (ROWS - 1, 0)[side]
        beside = [
            neighbours(
                lambda t, at=near + field * GROUP: halo[t, at : at + GROUP, :], lane_edge
            )
            for field in range(FIELDS)
        ]
        for tile in range(N_LON):
            zonal = halo[tile, near : near + GROUP, :]
            meridional = halo[tile, near + GROUP : near + 2 * GROUP, :]
            shares = weights(zonal, meridional, metric_edge)
            own_wind = state_ref[tile, pl.ds(GROUP * ROWS + own, GROUP, stride=ROWS), :]
            given = DIFFUSE + (-ADVECT, ADVECT)[side] * own_wind
            for field in range(FIELDS):
                own_rows = pl.ds(field * GROUP * ROWS + own, GROUP, stride=ROWS)
                here, east, west = beside[field](tile)
                outer = halo[tile, far + field * GROUP : far + (field + 1) * GROUP, :]
                inner = state_ref[tile, own_rows, :]
                north, south = ((outer, inner), (inner, outer))[side]
                result = stencil(here, east, west, north, south, shares)
                extra = turned(field, zonal, meridional, coriolis_edge)
                if extra is not None:
                    result = result + extra
                place = MAIN + side * PAIRS + field * GROUP
                result = jnp.where(exists > 0.5, result, 0.0)
                place = side * PAIRS + field * GROUP
                edge_ref[tile, place : place + GROUP, :] = result
                place = EDGE + place
                edge_ref[tile, place : place + GROUP, :] = given * here

    step_edge(0)
    step_edge(1)
    sums = fourier_sums(lambda tile: edge_ref[tile], analysis_ref)

    def emit(tile, smooth):
        edge = jnp.where(wanted_ref[MAIN:, :] == 1, smooth, edge_ref[tile])
        current_ref[tile, :MAIN, :] = inside_ref[tile]
        current_ref[tile, MAIN:, :] = edge[:EDGE]
        for side, own in enumerate((ROWS - 1, 0)):
            rows = pl.ds(own, PAIRS, stride=ROWS)
            place = EDGE + side * PAIRS
            current_ref[tile, rows, :] = current_ref[tile, rows, :] + edge[place : place + PAIRS]

    smooth_rows(band_ref[0], sums, both_edge_ref, synthesis_ref, emit)
    step_main(
        current_ref,
        stepped_ref,
        lambda tile, pair: current_ref[tile, pl.ds(MAIN + pair, 1), :],
        lambda tile, pair: current_ref[tile, pl.ds(MAIN + PAIRS + pair, 1), :],
        metric,
        coriolis,
    )
    filter_main(band_ref[0], stepped_ref, out_ref, wanted_ref, analysis_ref, synthesis_ref, both_ref)


def prepare_kernel(mixing_ref, map_ref, gain_ref, inverse_ref, order_ref):
    mix = mixing_ref[...]
    gain = jnp.zeros_like(mix)
    for level in range(LEVELS):
        inside = 1.0 if level in (0, LEVELS - 1) else 2.0
        inverse = 1.0 / (1.0 + inside * mix - mix * gain)
        gain = mix * inverse
        gain_ref[level] = gain
        inverse_ref[level] = inverse

    target = map_ref[...] // COLUMNS
    before = lax.broadcasted_iota(jnp.int32, (COLS, 2 * COLS), 0)
    after = lax.broadcasted_iota(jnp.int32, (COLS, 2 * COLS), 1)
    counter = jnp.where((before < after) | (after >= COLS), 1.0, 0.0).astype(BF16)
    block = lax.broadcasted_iota(jnp.int32, (BLOCKS, COLS), 0)
    sub = lax.broadcasted_iota(jnp.int32, (2 * ROWS, COLS), 0)
    earlier = jnp.zeros((BLOCKS, COLS), F32)
    one = jnp.ones((2 * ROWS, COLS), BF16)
    zero = jnp.zeros((2 * ROWS, COLS), BF16)
    for row in range(ROWS):
        goal = target[row : row + 1, :]
        chosen = jnp.where(block == goal, 1.0, 0.0)
        counted = jnp.dot(chosen.astype(BF16), counter, preferred_element_type=F32)
        rank = jnp.sum(chosen * (counted[:, :COLS] + earlier), axis=0, keepdims=True)
        earlier = earlier + counted[:, COLS:]
        seat = rank.astype(jnp.int32)
        pair = jnp.where(
            sub == seat, goal, jnp.where(sub == seat + ROWS, goal - 1, -1)
        ).astype(F32).astype(BF16)
        for even in range(0, BLOCKS, 2):
            order_ref[even * ROWS : (even + 2) * ROWS, row * COLS : (row + 1) * COLS] = jnp.where(
                pair == jnp.asarray(even, BF16), one, zero
            )


def physics_kernel(
    dyn_ref, mixing_ref, sun_ref, map_ref, gain_ref, inverse_ref, order_ref,
    stored_ref, send_ref, out_ref, heating_ref, table_ref, done_ref,
):
    zero = jnp.zeros((ROWS, COLS), F32)

    def forward(group, carry):
        for inner in range(GROUP):
            level = group * GROUP + inner
            gain = gain_ref[level]
            inverse = inverse_ref[level]
            carry = tuple(
                dyn_ref[group, (field * GROUP + inner) * ROWS : (field * GROUP + inner + 1) * ROWS, :]
                * inverse
                + gain * carry[field]
                for field in range(FIELDS)
            )
            for field in range(FIELDS):
                out_ref[field, level] = carry[field]
        return carry

    lax.fori_loop(0, N_LON, forward, (zero,) * FIELDS)
    sun = RADIATE * sun_ref[...]

    def backward(step, carry):
        group = N_LON - 1 - step
        for inner in reversed(range(GROUP)):
            level = group * GROUP + inner
            gain = gain_ref[level]
            carry = tuple(out_ref[field, level] + gain * carry[field] for field in range(FIELDS))
            warmed = carry[2] + sun * carry[3]
            out_ref[0, level] = carry[0]
            out_ref[1, level] = carry[1]
            out_ref[2, level] = warmed
            out_ref[3, level] = carry[3]
            at = (2 * GROUP + inner) * ROWS
            heating_ref[pl.ds(pl.multiple_of(level * ROWS, ROWS), ROWS), :] = (
                warmed - dyn_ref[group, at : at + ROWS, :]
            )
        return carry

    lax.fori_loop(0, N_LON, backward, (zero,) * FIELDS)

    store = pltpu.make_async_copy(out_ref, stored_ref, done_ref)
    store.start()
    slots = (map_ref[...] % COLUMNS).astype(F32)
    top = lax.broadcasted_iota(jnp.int32, (COLS - LEVELS, COLS), 0) == 0
    for row in range(ROWS):
        body = heating_ref[pl.ds(row, LEVELS, stride=ROWS), :]
        tail = jnp.where(top, slots[row : row + 1, :], 0.0)
        high, low = halves(jnp.concatenate([body, tail], axis=0))
        table_ref[:COLS, row * COLS : (row + 1) * COLS] = high
        table_ref[COLS:, row * COLS : (row + 1) * COLS] = low
    sent = lax.dot_general(
        order_ref[...], table_ref[...], (((1,), (1,)), ((), ())), preferred_element_type=F32
    )
    send_ref[...] = sent[:, :COLS] + sent[:, COLS:]
    store.wait()


def place_kernel(got_ref, out_ref):
    got = got_ref[...]
    slot = got[:, LEVELS : LEVELS + 1]
    column = lax.broadcasted_iota(jnp.int32, (COLUMNS, COLUMNS), 1).astype(F32)
    chosen = jnp.where(column == slot, 1.0, 0.0).astype(BF16)
    high, low = halves(got.T[:LEVELS])
    both = jnp.concatenate([high, low], axis=0)
    placed = jnp.dot(both, chosen, preferred_element_type=F32)
    out_ref[0] = placed[:LEVELS] + placed[LEVELS:]


def per_device(state, mixing, insolation, filter_rows, block_map):
    analysis, synthesis = (jnp.asarray(table) for table in fourier_tables())
    rows = jnp.asarray(row_tables())
    band = lax.axis_index("lat").astype(jnp.int32).reshape(1)

    state, band = lax.optimization_barrier((state, band))
    by_group, band_rows, wanted = call(
        gather_kernel, "gather",
        (
            ((N_LON, MAIN, COLS), F32),
            (rows.shape[1:], F32),
            ((MAIN + 2 * EDGE, COLS), jnp.int32),
        ),
        [pltpu.SMEM((N_LAT * ROWS,), jnp.int32), pltpu.SemaphoreType.DMA((FIELDS + 2,))], 1,
        band, state.reshape(FIELDS, N_LON, GROUP * ROWS, COLS), rows, filter_rows,
        scalars=1, taken=(0, 1, 2),
    )
    circles = lax.all_to_all(by_group, "lon", split_axis=0, concat_axis=0, tiled=True)
    edge = ((N_LON, EDGE, COLS), F32)
    to_near, to_far = call(pack_kernel, "pack", (edge, edge), [], 4, band, circles, scalars=1)
    near = lax.ppermute(to_near, "lat", [(i, i ^ 1) for i in range(N_LAT)])
    far = lax.ppermute(
        to_far, "lat", [(i, ((i + 1) ^ 1) - 1) for i in range(1, N_LAT - 1)]
    )
    (inside,) = call(
        inside_kernel, "inside", (((N_LON, MAIN, COLS), F32),),
        [pltpu.VMEM((N_LON, MAIN, COLS), F32), pltpu.VMEM((2 * MAIN, 2 * COLS), BF16)], 8,
        band, circles, band_rows, wanted, analysis, synthesis,
        scalars=1, after=(to_near, to_far),
    )
    levels = ((LEVELS, ROWS, COLS), F32)
    gain, inverse, order = call(
        prepare_kernel, "prepare", (levels, levels, ((COLUMNS, COLUMNS), BF16)), [], 4,
        mixing, block_map,
        after=(to_near,),
    )
    (dyn,) = call(
        dynamics_kernel,
        "dynamics",
        (((N_LON, MAIN, COLS), F32),),
        [
            pltpu.VMEM((N_LON, EDGE, COLS), F32),
            pltpu.VMEM((N_LON, EDGE, COLS), F32),
            pltpu.VMEM((N_LON, MAIN, COLS), F32),
            pltpu.VMEM((N_LON, MAIN + EDGE, COLS), F32),
            pltpu.VMEM((N_LON, 2 * EDGE, COLS), F32),
            pltpu.VMEM((4 * EDGE, 2 * COLS), BF16),
            pltpu.VMEM((2 * MAIN, 2 * COLS), BF16),
        ],
        16,
        band, circles, inside, near, far, band_rows, wanted, analysis, synthesis,
        scalars=1,
        after=(gain,),
    )
    columns = lax.all_to_all(dyn, "lon", split_axis=0, concat_axis=0, tiled=True)
    new_state, sent = call(
        physics_kernel,
        "physics",
        (((FIELDS, LEVELS, ROWS, COLS), F32), ((COLUMNS, COLS), F32)),
        [
            pltpu.VMEM((FIELDS, LEVELS, ROWS, COLS), F32),
            pltpu.VMEM((LEVELS * ROWS, COLS), F32),
            pltpu.VMEM((2 * COLS, COLUMNS), BF16),
            pltpu.SemaphoreType.DMA(()),
        ],
        12,
        columns, mixing, insolation, block_map, gain, inverse, order,
        left=(0,),
    )
    got = lax.all_to_all(
        sent.reshape(BLOCKS, ROWS, COLS), ("lat", "lon"), split_axis=0, concat_axis=0, tiled=True
    )
    (block_heating,) = call(
        place_kernel, "place", (((1, LEVELS, COLUMNS), F32),), [], 8, got.reshape(COLUMNS, COLS),
        stored=(0,),
    )
    return new_state, block_heating


def solution(mesh):
    in_specs = (P(None, None, "lat", "lon"), P("lat", "lon"), P("lat", "lon"), P(), P("lat", "lon"))
    out_specs = (P(None, None, "lat", "lon"), P(("lat", "lon"), None, None))
    return jax.shard_map(
        per_device, mesh=mesh, in_specs=in_specs, out_specs=out_specs, check_vma=False
    )
```
